32 devices in a mesh: mem: 8 (over z, y), lat: 4 (over x, core).
Axes of the slice: x: 2, y: 2, z: 4, core: 2. Of those that a mesh axis runs over, the one named last changes fastest.
Arguments:
- replica_variables: float32 [8, 4, 64, 4096], P('mem', None, 'lat'), may hold values from -40 to 40, as said below
- analysis: float32 [4, 64, 4096], P(None, 'lat'), may hold values from -4 to 4
- labels: int32 [64, 32], P('lat'), may hold values from 0 to 7, as said below
- pairing: int32 [8], replicated, may hold values from 0 to 7, as said below
Outputs:
- closing_ensemble_values: float32 [8, 4, 64, 4096], P('mem', None, 'lat')
- factor: float32 [8, 8], P('mem')
The draws below stay inside these ranges and needn't reach their ends.
Inputs may be any that keep to these rules, and one draw needn't show every extreme that they name: `replica_variables`: member fields; the spread of members differs across rows and columns. `labels`: every label value occurs at least once. pairing[pairing[m]] = m and pairing[m] != m for every member m.
All inputs are finite; a program needn't handle non-finite values.
Results may differ from the reference program's by a relative error of at most 0.00015.
Values sent between devices are 32-bit elements; how exact they have to be, the bound alone decides.
A program may use at most 64 MiB of HBM per device.

```python
import jax
import jax.numpy as jnp
from jax import lax

LON = 4096
TILE = 128
REGIONS = 8
STEPS = 3
MEMBERS = 8
NLAT = 64


def draw_replica_variables(key, part):
    keys = jax.random.split(key, 3)
    rows = jnp.arange(NLAT).astype(jnp.float32)
    rising = jnp.exp(jnp.log(3.0) * rows / max(NLAT - 1, 1))
    row_scale = rising * jnp.exp(jax.random.uniform(keys[0], (NLAT,), minval=0.0, maxval=1.15))
    col_scale = jnp.exp(jax.random.uniform(keys[1], (LON,), minval=0.0, maxval=1.15))
    scale = 0.05 * row_scale[:, None] * col_scale[None, :]
    base = jax.random.normal(keys[2], (MEMBERS, 4, NLAT, LON))
    return (base * scale).astype(jnp.float32)


def draw_labels(key, part):
    first_key, second_key = jax.random.split(key, 2)
    tiles = LON // TILE
    base = jax.random.randint(first_key, (NLAT * tiles,), 0, REGIONS).astype(jnp.int32)
    places = jax.random.permutation(second_key, NLAT * tiles)[:REGIONS]
    base = base.at[places].set(jnp.arange(REGIONS, dtype=jnp.int32))
    return base.reshape(NLAT, tiles).astype(jnp.int32)


def draw_pairing(key, part):
    order = jax.random.permutation(key, MEMBERS).astype(jnp.int32)
    evens = order[0::2]
    odds = order[1::2]
    partner = jnp.zeros((MEMBERS,), jnp.int32).at[evens].set(odds).at[odds].set(evens)
    return partner.astype(jnp.int32)


def level_of(rng, shape, cuts, low, high):
    gain = 1.0
    for position, blocks in cuts:
        draws = jax.random.uniform(jax.random.fold_in(jax.random.fold_in(rng, 6), position), (blocks,), jnp.float32, low / len(cuts), high / len(cuts))
        gain = gain * jnp.repeat(jnp.exp(draws), shape[position] // blocks).reshape((-1,) + (1,) * (len(shape) - 1 - position))
    return gain


def gaussian(rng, extent, scale, reach, cuts=(), held_as=jnp.bfloat16):
    loudness = level_of(rng, extent, cuts, -0.22, 0.18) if cuts else 1.0
    values = jax.random.normal(rng, extent, jnp.float32) * scale * loudness
    return jnp.minimum(jnp.maximum(values, -reach), reach).astype(held_as)


def setup_inputs(seed: int = 0) -> dict:
    key_of = jax.random.split(jax.random.key(seed), 5)
    return {
        "replica_variables": draw_replica_variables(jax.random.fold_in(key_of[4], 71), 0),
        "analysis": gaussian(key_of[1], (4, NLAT, LON), 0.5, 4.0, ((1, 4),), jnp.float32),
        "labels": draw_labels(jax.random.fold_in(key_of[4], 71), 0),
        "pairing": draw_pairing(jax.random.fold_in(key_of[4], 71), 0),
    }


grav_coef = 0.1
depth_coef = 0.1
advect_coef = 0.05
diffuse_coef = 0.05
coriolis_coef = 0.05
target_size = 0.5
small_eps = 1e-06

def diff_lon(field):
    return jnp.roll(field, -1, axis=-1) - jnp.roll(field, 1, axis=-1)

def trimmed_latitude_lines(field, have, want, offset=0):
    margin = have - want
    total = field.shape[-2]
    return field[..., margin + offset:total - margin + offset, :]

def model_step(extended, have, coriolis, height_rim):
    height = extended[:, 0]
    zonal = extended[:, 1]
    meridional = extended[:, 2]
    tracer = extended[:, 3]
    inner = have - 1
    new_height = trimmed_latitude_lines(height, have, inner) - depth_coef * (diff_lon(trimmed_latitude_lines(zonal, have, inner)) + trimmed_latitude_lines(meridional, have, inner, 1) - trimmed_latitude_lines(meridional, have, inner, -1))
    new_zonal = trimmed_latitude_lines(zonal, have, inner) + trimmed_latitude_lines(coriolis, have, inner) * trimmed_latitude_lines(meridional, have, inner) - grav_coef * diff_lon(new_height)
    padded_height, height_have = height_rim(new_height, inner)
    outer = height_have - 1
    zonal_out = trimmed_latitude_lines(new_zonal, inner, outer)
    new_meridional = trimmed_latitude_lines(meridional, have, outer) - trimmed_latitude_lines(coriolis, have, outer) * zonal_out - grav_coef * (trimmed_latitude_lines(padded_height, height_have, outer, 1) - trimmed_latitude_lines(padded_height, height_have, outer, -1))
    centre = trimmed_latitude_lines(tracer, have, outer)
    upper = trimmed_latitude_lines(tracer, have, outer, 1)
    lower = trimmed_latitude_lines(tracer, have, outer, -1)
    new_tracer = centre - advect_coef * (zonal_out * diff_lon(centre) + new_meridional * (upper - lower)) + diffuse_coef * (jnp.roll(centre, -1, axis=-1) + jnp.roll(centre, 1, axis=-1) + upper + lower - 4.0 * centre)
    quantity_bundle = jnp.stack([trimmed_latitude_lines(padded_height, height_have, outer), zonal_out, new_meridional, new_tracer], axis=1)
    return (quantity_bundle, outer)

def height_with_halo(new_height, have):
    return (jnp.pad(new_height, ((0, 0), (1, 1), (0, 0))), have + 1)

def predicted_flow(quantity_bundle):
    rows_all = quantity_bundle.shape[2]
    global_rows = jnp.arange(-1, rows_all + 1).astype(jnp.float32)
    coriolis = (coriolis_coef * (2.0 * (global_rows + 0.5) / rows_all - 1.0))[:, None]
    for index in range(STEPS):
        extended = jnp.pad(quantity_bundle, ((0, 0), (0, 0), (1, 1), (0, 0)))
        quantity_bundle, _ = model_step(extended, 1, coriolis, height_with_halo)
    return quantity_bundle

def reference(replica_variables, analysis, labels, pairing):
    leading_replica = predicted_flow(replica_variables)
    partner = leading_replica[pairing]
    spread = 0.5 * (leading_replica - partner)
    energy = 0.5 * lax.optimization_barrier(jnp.sum(spread * spread, axis=1))
    padded = jnp.pad(energy, ((0, 0), (1, 1), (0, 0)))
    smoothed_field = 0.25 * (padded[:, 2:] + 2.0 * energy + padded[:, :-2])
    members, rows_all, width = smoothed_field.shape
    tiles = width // TILE
    tile_sums = smoothed_field.reshape(members, rows_all, tiles, TILE).sum(-1)
    onehot = (labels[..., None] == jnp.arange(REGIONS, dtype=jnp.int32)).astype(jnp.float32)
    region_sum = jnp.einsum('mrt,rtk->mk', tile_sums, onehot, precision=lax.Precision.HIGHEST)
    cells = onehot.sum((0, 1)) * TILE
    factor = target_size / jnp.sqrt(region_sum / cells + small_eps)
    cell_factor = jnp.einsum('mk,rtk->mrt', factor, onehot, precision=lax.Precision.HIGHEST)
    scaled = (spread.reshape(members, 4, rows_all, tiles, TILE) * cell_factor[:, None, :, :, None]).reshape(spread.shape)
    central_latitude_lines = analysis[None] + scaled
    closing_ensemble_values = predicted_flow(central_latitude_lines)
    return (closing_ensemble_values, factor)
```

```python
import functools

import jax
import jax.numpy as jnp
from jax import lax
from jax.experimental import pallas as pl
from jax.experimental.pallas import tpu as pltpu
from jax.sharding import PartitionSpec as P

MESH = pl.DeviceIdType.MESH
TILE = 128
REGIONS = 8
STEPS = 3
MAX_BRANCHES = 28
MAX_LEVELS = 4
OPEN_VMEM = 8 * 2**20
HALO = 2 * STEPS
VMEM_LIMIT = 24 * 2**20
FIELDS = 4
REACH = (2 * STEPS - 1, 2 * STEPS - 1, 2 * STEPS, STEPS)


grav_coef = 0.1
depth_coef = 0.1
advect_coef = 0.05
diffuse_coef = 0.05
coriolis_coef = 0.05
target_size = 0.5
small_eps = 1e-06


def shift_lon(plane):
    sub = plane.shape[0]
    lane = lax.broadcasted_iota(jnp.int32, plane.shape, 1)
    east = pltpu.roll(plane, TILE - 1, 1)
    east = jnp.where(lane == TILE - 1, pltpu.roll(east, sub - 1, 0), east)
    west = pltpu.roll(plane, 1, 1)
    west = jnp.where(lane == 0, pltpu.roll(west, 1, 0), west)
    return east, west


def diff_lon(plane):
    east, west = shift_lon(plane)
    return east - west


def run_steps(state, buf, spare, local_rows, sub, start, rows_all):
    extent = local_rows + 2 * HALO

    def at(field, e):
        return pl.ds((field * extent + e) * sub, sub)

    def masked(e, plane):
        if HALO <= e < HALO + local_rows:
            return plane
        row = start + (e - HALO)
        return jnp.where((row >= 0) & (row < rows_all), 1.0, 0.0).astype(jnp.float32) * plane

    def coriolis(e):
        row = (start + (e - HALO)).astype(jnp.float32)
        return coriolis_coef * (2.0 * (row + 0.5) / rows_all - 1.0)

    tracer_source, source_field = state, 3
    for step in range(STEPS):
        margin = 2 * (STEPS - 1 - step)
        narrow = STEPS - 1 - step
        target, target_field = (spare, 0) if step % 2 == 0 else (buf, 3)
        own = (HALO, HALO + local_rows)
        for e in range(own[0] - margin - 1, own[1] + margin + 1):
            divergence = diff_lon(state[at(1, e), :]) + state[at(2, e + 1), :] - state[at(2, e - 1), :]
            buf[at(0, e), :] = masked(e, state[at(0, e), :] - depth_coef * divergence)
        for e in range(own[0] - margin, own[1] + margin):
            f = coriolis(e)
            v = state[at(2, e), :]
            u1 = state[at(1, e), :] + f * v - grav_coef * diff_lon(buf[at(0, e), :])
            slope = buf[at(0, e + 1), :] - buf[at(0, e - 1), :]
            buf[at(1, e), :] = u1
            buf[at(2, e), :] = masked(e, v - f * u1 - grav_coef * slope)
        for e in range(own[0] - narrow, own[1] + narrow):
            q = tracer_source[at(source_field, e), :]
            upper = tracer_source[at(source_field, e + 1), :]
            lower = tracer_source[at(source_field, e - 1), :]
            east, west = shift_lon(q)
            advected = buf[at(1, e), :] * (east - west) + buf[at(2, e), :] * (upper - lower)
            spreading = east + west + upper + lower - 4.0 * q
            target[at(target_field, e), :] = masked(e, q - advect_coef * advected + diffuse_coef * spreading)
        state = buf
        tracer_source, source_field = target, target_field
    return [(buf, 0), (buf, 1), (buf, 2), (tracer_source, source_field)]


def pairs_of(size):
    return [(a, b) for a in range(size) for b in range(a + 1, size)]


def pair_index(pairing_ref):
    size = pairing_ref.shape[0]
    me = lax.axis_index("mem")
    partner = pairing_ref[me]
    low, high = jnp.minimum(me, partner), jnp.maximum(me, partner)
    return low * (2 * size - low - 1) // 2 + high - low - 1


def steps_kernel(size, local_rows, sub, as_rows, *refs):
    extent = local_rows + 2 * HALO
    if as_rows:
        state_ref, factor_ref, out_ref, factor_out, buf, spare = refs
        factor_out[...] = factor_ref[...]
    else:
        state_ref, pairing_ref, out_ref, index_ref, buf, spare = refs
        index_ref[0, 0] = pair_index(pairing_ref)
    lat = lax.axis_index("lat")
    fields = run_steps(state_ref, buf, spare, local_rows, sub, lat * local_rows, local_rows * size)
    for field, (ref, place) in enumerate(fields):
        if not as_rows:
            for tile in range(local_rows * sub // 8):
                column = (field * local_rows * sub // 8 + tile) * TILE
                out_ref[:, column : column + TILE] = ref[pl.ds((place * extent + HALO) * sub + tile * 8, 8), :]
            continue
        for row in range(0, local_rows, 8):
            for t in range(sub):
                first = (place * extent + HALO + row) * sub + t
                out_ref[field, row : row + 8, t * TILE : (t + 1) * TILE] = ref[pl.ds(first, 8, stride=sub), :]


def halo_copies(buf, local_rows, sub, lat, size, send_sem, recv_sem):
    extent = local_rows + 2 * HALO
    mem = lax.axis_index("mem")
    copies = []
    for side, peer in ((0, lat - 1), (1, lat + 1)):
        group = []
        for field in range(FIELDS):
            reach = REACH[field]
            source = HALO if side == 0 else HALO + local_rows - reach
            target = HALO + local_rows if side == 0 else HALO - reach
            group.append(
                pltpu.make_async_remote_copy(
                    src_ref=buf.at[pl.ds((field * extent + source) * sub, reach * sub), :],
                    dst_ref=buf.at[pl.ds((field * extent + target) * sub, reach * sub), :],
                    send_sem=send_sem.at[side, field],
                    recv_sem=recv_sem.at[side, field],
                    device_id=(mem, peer),
                    device_id_type=MESH,
                )
            )
        copies.append(group)
    return copies


def clear_outside(buf, local_rows, sub, lat, size):
    extent = local_rows + 2 * HALO
    zeros = jnp.zeros((HALO * sub, TILE), jnp.float32)

    @pl.when(lat == 0)
    def _():
        for field in range(FIELDS):
            buf[pl.ds(field * extent * sub, HALO * sub), :] = zeros

    @pl.when(lat == size - 1)
    def _():
        for field in range(FIELDS):
            buf[pl.ds((field * extent + HALO + local_rows) * sub, HALO * sub), :] = zeros


def start_halo(copies, lat, size):
    for side, has in ((0, lat > 0), (1, lat < size - 1)):

        @pl.when(has)
        def _(side=side):
            for copy in copies[side]:
                copy.start()


def finish_halo(copies, lat, size):
    for side, has in ((0, lat > 0), (1, lat < size - 1)):

        @pl.when(has)
        def _(side=side):
            for copy in copies[side]:
                copy.wait_send()
            for copy in copies[1 - side]:
                copy.wait_recv()


def planes_from_rows(source, buf, local_rows, sub, fields=range(FIELDS)):
    extent = local_rows + 2 * HALO
    for field in fields:
        for row in range(0, local_rows, 8):
            for t in range(sub):
                first = (field * extent + HALO + row) * sub + t
                buf[pl.ds(first, 8, stride=sub), :] = source[field, row : row + 8, t * TILE : (t + 1) * TILE]


def first_kernel(size, local_rows, sub, x_ref, lab_ref, buf, edge_ref, rows, load_sem, send_sem, recv_sem, lab_send, lab_recv):
    lat = lax.axis_index("lat")
    mem = lax.axis_index("mem")
    barrier = pltpu.get_barrier_semaphore()
    for peer, has in ((lat - 1, lat > 0), (lat + 1, lat < size - 1)):

        @pl.when(has)
        def _(peer=peer):
            pl.semaphore_signal(barrier, inc=1, device_id=(mem, peer), device_id_type=MESH)

    loads = [pltpu.make_async_copy(x_ref.at[f], rows.at[f], load_sem.at[f]) for f in range(FIELDS)]
    for load in loads:
        load.start()
    clear_outside(buf, local_rows, sub, lat, size)
    none = jnp.full((sub, TILE), -1.0, jnp.float32)

    @pl.when(lat == 0)
    def _():
        edge_ref[0] = none

    @pl.when(lat == size - 1)
    def _():
        edge_ref[1] = none

    inner = (lat > 0) & (lat < size - 1)

    @pl.when(inner)
    def _():
        pl.semaphore_wait(barrier, 2)

    @pl.when(jnp.logical_not(inner))
    def _():
        pl.semaphore_wait(barrier, 1)

    copies = halo_copies(buf, local_rows, sub, lat, size, send_sem, recv_sem)
    for side, peer in ((0, lat - 1), (1, lat + 1)):
        row = 0 if side == 0 else local_rows - 1
        copies[side].append(
            pltpu.make_async_remote_copy(
                src_ref=lab_ref.at[row],
                dst_ref=edge_ref.at[1 - side],
                send_sem=lab_send.at[side],
                recv_sem=lab_recv.at[side],
                device_id=(mem, peer),
                device_id_type=MESH,
            )
        )
    for field in range(FIELDS + 1):
        if field < FIELDS:
            loads[field].wait()
            planes_from_rows(rows, buf, local_rows, sub, (field,))
        start_halo([side[field : field + 1] for side in copies], lat, size)
    finish_halo(copies, lat, size)


def second_kernel(
    size, local_rows, sub, first_ref, partner_ref, analysis_ref, lab_ref, edge_ref, buf, factor_ref,
    spread, sums, send_sem, recv_sem, sum_send, sum_recv,
):
    lat = lax.axis_index("lat")
    mem = lax.axis_index("mem")
    extent = local_rows + 2 * HALO
    barrier = pltpu.get_barrier_semaphore()
    for hop in range(1, size):
        pl.semaphore_signal(barrier, inc=1, device_id=(mem, lax.rem(lat + hop, size)), device_id_type=MESH)

    def fold(plane):
        total = plane[0:8]
        for i in range(8, sub, 8):
            total = total + plane[i : i + 8]
        return total

    energies = [jnp.zeros((8, TILE), jnp.float32) for _ in range(REGIONS)]
    counts = [jnp.zeros((8, TILE), jnp.float32) for _ in range(REGIONS)]

    def accumulate(row, carry):
        energies, counts = carry
        total = jnp.zeros((sub, TILE), jnp.float32)
        for field in range(FIELDS):
            parts = []
            for i in range(sub // 8):
                column = ((field * local_rows + row) * (sub // 8) + i) * TILE
                place = pl.ds(pl.multiple_of(column, TILE), TILE)
                parts.append(first_ref[:, place] - partner_ref[:, place])
            half = 0.5 * jnp.concatenate(parts, axis=0)
            spread[field, row] = half
            total = total + half * half
        quarter = 0.125 * total
        here = lab_ref[row]
        before = jnp.where(row == 0, edge_ref[0], lab_ref[jnp.maximum(row - 1, 0)])
        after = jnp.where(row == local_rows - 1, edge_ref[1], lab_ref[jnp.minimum(row + 1, local_rows - 1)])
        new_energies, new_counts = [], []
        for k in range(REGIONS):
            kept = jnp.where(here == k, 1.0, 0.0)
            weight = 2.0 * kept + jnp.where(before == k, 1.0, 0.0) + jnp.where(after == k, 1.0, 0.0)
            new_energies.append(energies[k] + fold(quarter * weight))
            new_counts.append(counts[k] + fold(kept))
        return new_energies, new_counts

    energies, counts = lax.fori_loop(0, local_rows, accumulate, (energies, counts))
    for k in range(REGIONS):
        sums[0, k : k + 1, :] = jnp.sum(energies[k], axis=0, keepdims=True)
        sums[0, REGIONS + k : REGIONS + k + 1, :] = jnp.sum(counts[k], axis=0, keepdims=True)

    pl.semaphore_wait(barrier, size - 1)
    sends = []
    for hop in range(1, size):
        sends.append(
            pltpu.make_async_remote_copy(
                src_ref=sums.at[0],
                dst_ref=sums.at[hop],
                send_sem=sum_send.at[hop],
                recv_sem=sum_recv.at[hop],
                device_id=(mem, lax.rem(lat + hop, size)),
                device_id_type=MESH,
            )
        )
    for copy in sends:
        copy.start()
    clear_outside(buf, local_rows, sub, lat, size)
    planes_from_rows(analysis_ref, buf, local_rows, sub)
    for copy in sends:
        copy.wait()
    total = sums[0]
    for hop in range(1, size):
        total = total + sums[hop]
    total = jnp.sum(total, axis=1, keepdims=True)
    factor = target_size / jnp.sqrt(total[:REGIONS] / total[REGIONS:] + small_eps)
    wide = jnp.broadcast_to(factor, (REGIONS, TILE))
    diagonal = lax.broadcasted_iota(jnp.int32, (REGIONS, TILE), 0) == lax.broadcasted_iota(
        jnp.int32, (REGIONS, TILE), 1
    )
    factor_ref[...] = jnp.sum(jnp.where(diagonal, wide, 0.0), axis=0, keepdims=True)[:, :REGIONS]
    lanes = [jnp.broadcast_to(wide[k : k + 1], (sub, TILE)) for k in range(REGIONS)]

    def middle(row, carry):
        here = lab_ref[row]
        scale = lanes[0]
        for k in range(1, REGIONS):
            scale = jnp.where(here == k, lanes[k], scale)
        for field in range(FIELDS):
            place = pl.ds(pl.multiple_of((field * extent + HALO + row) * sub, sub), sub)
            buf[place, :] = buf[place, :] + scale * spread[field, row]
        return carry

    lax.fori_loop(0, local_rows, middle, 0)
    copies = halo_copies(buf, local_rows, sub, lat, size, send_sem, recv_sem)
    start_halo(copies, lat, size)
    finish_halo(copies, lat, size)


def partner_fields(fields, pairing, index):
    pairs = pairs_of(lax.axis_size("mem"))
    if len(pairs) > MAX_BRANCHES:
        piece = lax.all_gather(fields, "mem", axis=0)
        return lax.dynamic_index_in_dim(piece, pairing[lax.axis_index("mem")], 0, keepdims=False)
    branches = [
        functools.partial(lax.ppermute, axis_name="mem", perm=[(a, b), (b, a)]) for a, b in pairs
    ]
    return lax.switch(index, branches, fields)


def local(replica_variables, analysis, labels, pairing):
    size = lax.axis_size("lat")
    fields, local_rows, width = analysis.shape
    sub = width // TILE
    extent = local_rows + 2 * HALO
    wide = jax.ShapeDtypeStruct((8, fields * local_rows * width // 8), jnp.float32)
    extended = jax.ShapeDtypeStruct((fields * extent * sub, TILE), jnp.float32)
    edges = jax.ShapeDtypeStruct((2, sub, TILE), jnp.float32)
    factors = jax.ShapeDtypeStruct((1, REGIONS), jnp.float32)
    label_planes = jnp.broadcast_to(labels.astype(jnp.float32)[..., None], (local_rows, sub, TILE))
    whole = pl.BlockSpec(memory_space=pltpu.VMEM)
    buffers = [
        pltpu.VMEM((fields * extent * sub, TILE), jnp.float32),
        pltpu.VMEM((extent * sub, TILE), jnp.float32),
    ]
    halo_sems = [pltpu.SemaphoreType.DMA((2, fields)), pltpu.SemaphoreType.DMA((2, fields))]
    state, edge = pl.pallas_call(
        functools.partial(first_kernel, size, local_rows, sub),
        out_shape=(extended, edges),
        in_specs=[pl.BlockSpec(memory_space=pltpu.HBM), whole],
        out_specs=(whole, whole),
        scratch_shapes=[pltpu.VMEM(analysis.shape, jnp.float32), pltpu.SemaphoreType.DMA((fields,))]
        + halo_sems
        + [pltpu.SemaphoreType.DMA((2,)), pltpu.SemaphoreType.DMA((2,))],
        compiler_params=pltpu.CompilerParams(collective_id=0, has_side_effects=True, vmem_limit_bytes=VMEM_LIMIT),
    )(replica_variables[0], label_planes)
    smem = pl.BlockSpec(memory_space=pltpu.SMEM)
    first, index = pl.pallas_call(
        functools.partial(steps_kernel, size, local_rows, sub, False),
        out_shape=(wide, jax.ShapeDtypeStruct((1, 1), jnp.int32)),
        in_specs=[whole, smem],
        out_specs=(whole, smem),
        scratch_shapes=buffers,
        compiler_params=pltpu.CompilerParams(vmem_limit_bytes=VMEM_LIMIT),
    )(state, pairing)
    partner = partner_fields(first, pairing, index[0, 0])
    state, factor = pl.pallas_call(
        functools.partial(second_kernel, size, local_rows, sub),
        out_shape=(extended, factors),
        in_specs=[whole] * 5,
        out_specs=(whole, whole),
        scratch_shapes=[
            pltpu.VMEM((fields, local_rows, sub, TILE), jnp.float32),
            pltpu.VMEM((size, 2 * REGIONS, TILE), jnp.float32),
        ]
        + halo_sems
        + [pltpu.SemaphoreType.DMA((size,)), pltpu.SemaphoreType.DMA((size,))],
        compiler_params=pltpu.CompilerParams(collective_id=1, has_side_effects=True, vmem_limit_bytes=VMEM_LIMIT),
    )(first, partner, analysis, label_planes, edge)
    closing, factor = pl.pallas_call(
        functools.partial(steps_kernel, size, local_rows, sub, True),
        out_shape=(jax.ShapeDtypeStruct(analysis.shape, jnp.float32), factors),
        in_specs=[whole] * 2,
        out_specs=(whole, whole),
        scratch_shapes=buffers,
        compiler_params=pltpu.CompilerParams(vmem_limit_bytes=VMEM_LIMIT),
    )(state, factor)
    return (closing[None], factor)


CLASS_ID = 2
COLUMNS = 2
CHUNKS = 2
PAIR_VMEM = 12 * 2**20


def matchings(items):
    if not items:
        return [()]
    head, found = items[0], []
    for i in range(1, len(items)):
        for rest in matchings(items[1:i] + items[i + 1 :]):
            found.append(((head, items[i]),) + rest)
    return found


def level_edges(matching):
    return tuple(sorted(tuple(sorted((a // COLUMNS, b // COLUMNS))) for a, b in matching))


def level_patterns(size):
    return sorted({level_edges(m) for m in matchings(tuple(range(size)))})


def slot_tables(edges, levels):
    peer = [[z, z] for z in range(levels)]
    slot = [[0, 1] for _ in range(levels)]
    moves = [0] * levels
    used = [0] * levels
    for a, b in edges:
        if a == b:
            continue
        i, j = used[a], used[b]
        used[a] += 1
        used[b] += 1
        peer[a][i], slot[a][i] = b, j
        peer[b][j], slot[b][j] = a, i
        moves[a] = moves[b] = 1
    return peer, slot, moves


def pattern_index(patterns, pairing_ref):
    members = pairing_ref.shape[0]
    levels = members // COLUMNS
    level = [lax.div(pairing_ref[m], COLUMNS) for m in range(members)]
    count = {}
    for a in range(levels):
        for b in range(a + 1, levels):
            count[a, b] = sum(jnp.where(level[a * COLUMNS + i] == b, 1, 0) for i in range(COLUMNS))
    index = jnp.int32(0)
    for k, edges in enumerate(patterns):
        good = None
        for pair, n in count.items():
            same = n == sum(e == pair for e in edges)
            good = same if good is None else good & same
        index = jnp.where(good, k, index)
    return index


def lookup(index, table):
    value = jnp.int32(table[0])
    for k, entry in enumerate(table):
        if k and entry != table[0]:
            value = jnp.where(index == k, entry, value)
    return value


def opening_kernel(size, local_rows, sub, x_ref, buf, rows, load_sem, send_sem, recv_sem):
    lat = lax.axis_index("lat")
    mem = lax.axis_index("mem")
    barrier = pltpu.get_barrier_semaphore()
    for peer, has in ((lat - 1, lat > 0), (lat + 1, lat < size - 1)):

        @pl.when(has)
        def _(peer=peer):
            pl.semaphore_signal(barrier, inc=1, device_id=(mem, peer), device_id_type=MESH)

    loads = [pltpu.make_async_copy(x_ref.at[f], rows.at[f], load_sem.at[f]) for f in range(FIELDS)]
    for load in loads:
        load.start()
    clear_outside(buf, local_rows, sub, lat, size)
    inner = (lat > 0) & (lat < size - 1)

    @pl.when(inner)
    def _():
        pl.semaphore_wait(barrier, 2)

    @pl.when(jnp.logical_not(inner))
    def _():
        pl.semaphore_wait(barrier, 1)

    copies = halo_copies(buf, local_rows, sub, lat, size, send_sem, recv_sem)
    for field in range(FIELDS):
        loads[field].wait()
        planes_from_rows(rows, buf, local_rows, sub, (field,))
        start_halo([side[field : field + 1] for side in copies], lat, size)
    finish_halo(copies, lat, size)


def first_steps_kernel(size, local_rows, sub, patterns, state_ref, pairing_ref, out_ref, index_ref, buf, spare):
    extent = local_rows + 2 * HALO
    index_ref[0, 0] = pattern_index(patterns, pairing_ref)
    lat = lax.axis_index("lat")
    fields = run_steps(state_ref, buf, spare, local_rows, sub, lat * local_rows, local_rows * size)
    for field, (ref, place) in enumerate(fields):
        for tile in range(local_rows * sub // 8):
            out_ref[pl.ds((field * local_rows * sub) + tile * 8, 8), :] = ref[
                pl.ds((place * extent + HALO) * sub + tile * 8, 8), :
            ]


def plane(sub, index):
    return pl.ds(pl.multiple_of(index * sub, sub), sub)


def fold(block):
    total = block[0:8]
    for i in range(8, block.shape[0], 8):
        total = total + block[i : i + 8]
    return total


def pair_kernel(
    tables, size, local_rows, sub,
    first_ref, analysis_ref, lab_ref, pairing_ref,
    partner, state, labels, weights, tally,
    av, near, send, came, onward,
    load_sem, near_send, near_recv, z_send, z_recv, last_send, last_recv,
    ana_send, ana_recv, lab_send, lab_recv,
):
    lat = lax.axis_index("lat")
    mem = lax.axis_index("mem")
    z, y = lax.div(mem, COLUMNS), lax.rem(mem, COLUMNS)
    peer_table, slot_table, moves_table = tables
    levels = len(moves_table)
    half = local_rows // COLUMNS
    deep = half // CHUNKS
    block = deep * sub
    chunks = FIELDS * CHUNKS
    extent = local_rows + 2 * HALO
    other = (z * COLUMNS + 1 - y, lat)
    peers = [lookup(z, [peer_table[k][j] for k in range(levels)]) for j in range(2)]
    slots = [lookup(z, [slot_table[k][j] for k in range(levels)]) for j in range(2)]
    moves = lookup(z, moves_table) == 1

    load = pltpu.make_async_copy(analysis_ref, av, load_sem.at[0])
    load.start()
    barrier = pltpu.get_barrier_semaphore()
    pl.semaphore_signal(barrier, inc=1, device_id=other, device_id_type=MESH)
    for hop in range(1, size):
        pl.semaphore_signal(barrier, inc=1, device_id=(mem, lax.rem(lat + hop, size)), device_id_type=MESH)

    @pl.when(moves)
    def _():
        for j in range(2):
            pl.semaphore_signal(barrier, inc=1, device_id=(peers[j] * COLUMNS + y, lat), device_id_type=MESH)

    @pl.when(moves)
    def _():
        pl.semaphore_wait(barrier, size + 2)

    @pl.when(jnp.logical_not(moves))
    def _():
        pl.semaphore_wait(barrier, size)

    def rows_of(c, column):
        field, part = lax.div(c, CHUNKS), lax.rem(c, CHUNKS)
        return pl.ds(pl.multiple_of((field * local_rows + column * half + part * deep) * sub, sub), block)

    def near_copy(c):
        return pltpu.make_async_remote_copy(
            src_ref=first_ref.at[rows_of(c, 1 - y), :],
            dst_ref=near.at[c],
            send_sem=near_send.at[c],
            recv_sem=near_recv.at[c],
            device_id=other,
            device_id_type=MESH,
        )

    def cross_copy(c, j, slot):
        return pltpu.make_async_remote_copy(
            src_ref=send.at[j, c],
            dst_ref=came.at[slot, c],
            send_sem=z_send.at[j, c],
            recv_sem=z_recv.at[slot, c],
            device_id=(peers[j] * COLUMNS + y, lat),
            device_id_type=MESH,
        )

    def last_copy(c):
        return pltpu.make_async_remote_copy(
            src_ref=onward.at[c],
            dst_ref=partner.at[rows_of(c, y), :],
            send_sem=last_send.at[c],
            recv_sem=last_recv.at[c],
            device_id=other,
            device_id_type=MESH,
        )

    def start_near(c, carry):
        near_copy(c).start()
        return carry

    lax.fori_loop(0, chunks, start_near, 0)

    pick = [pairing_ref[z * COLUMNS + i] for i in range(COLUMNS)]
    pick_level = [lax.div(p, COLUMNS) for p in pick]
    first_slot_item = jnp.where(pick_level[0] == peers[0], 0, 1)
    here_level = jnp.where(y == 0, pick_level[0], pick_level[1])
    here_column = lax.rem(jnp.where(y == 0, pick[0], pick[1]), COLUMNS)
    keep_slot = jnp.where(peers[0] == peers[1], here_column, jnp.where(here_level == peers[0], 0, 1))
    own_first = jnp.full((block, TILE), first_slot_item, jnp.int32) == y
    keep_first = jnp.full((block, TILE), keep_slot, jnp.int32) == 0

    clear_outside(state, local_rows, sub, lat, size)
    none = jnp.full((HALO * sub, TILE), -1.0, jnp.float32)

    @pl.when(lat == 0)
    def _():
        labels[pl.ds(0, HALO * sub), :] = none

    @pl.when(lat == size - 1)
    def _():
        labels[pl.ds((HALO + local_rows) * sub, HALO * sub), :] = none

    diagonal = lax.broadcasted_iota(jnp.int32, (sub, sub), 0) == lax.broadcasted_iota(jnp.int32, (sub, sub), 1)
    load.wait()

    def lay_out(c):
        for part in range(CHUNKS):
            block_row = part * 8

            def put(t, carry, block_row=block_row):
                for i in range(sub // CHUNKS):
                    tile = lax.rem(c, CHUNKS) * (sub // CHUNKS) + i
                    field = lax.div(c, CHUNKS)
                    first = (field * extent + HALO + block_row) * sub + tile
                    state[pl.ds(first, 8, stride=sub), :] = av[
                        field, block_row : block_row + 8, pl.ds(pl.multiple_of(tile * TILE, TILE), TILE)
                    ]
                return carry

            put(0, 0)
        for i in range(local_rows // chunks):
            row = c * (local_rows // chunks) + i
            line = jnp.broadcast_to(lab_ref[pl.ds(row, 1), :].astype(jnp.float32), (sub, sub))
            column = jnp.sum(jnp.where(diagonal, line, 0.0), axis=1, keepdims=True)
            labels[plane(sub, HALO + row), :] = jnp.broadcast_to(column, (sub, TILE))

    def cross(c, carry):
        lay_out(c)
        near_copy(c).wait_recv()

        @pl.when(moves)
        def _():
            a = first_ref[rows_of(c, y), :]
            b = near[c]
            send[0, c] = jnp.where(own_first, a, b)
            send[1, c] = jnp.where(own_first, b, a)
            for j in range(2):
                cross_copy(c, j, slots[j]).start()

        return carry

    lax.fori_loop(0, chunks, cross, 0)
    ana_copies = halo_copies(state, local_rows, sub, lat, size, ana_send, ana_recv)
    lab_copies = [
        [
            pltpu.make_async_remote_copy(
                src_ref=labels.at[pl.ds(HALO * sub if side == 0 else local_rows * sub, HALO * sub), :],
                dst_ref=labels.at[pl.ds((HALO + local_rows) * sub if side == 0 else 0, HALO * sub), :],
                send_sem=lab_send.at[side],
                recv_sem=lab_recv.at[side],
                device_id=(mem, peer),
                device_id_type=MESH,
            )
        ]
        for side, peer in ((0, lat - 1), (1, lat + 1))
    ]
    start_halo(lab_copies, lat, size)
    start_halo(ana_copies, lat, size)

    def forward(c, carry):
        @pl.when(moves)
        def _():
            for j in range(2):
                cross_copy(c, j, j).wait()
            a = came[0, c]
            b = came[1, c]
            onward[c] = jnp.where(keep_first, b, a)
            partner[rows_of(c, y), :] = jnp.where(keep_first, a, b)

        @pl.when(jnp.logical_not(moves))
        def _():
            onward[c] = first_ref[rows_of(c, y), :]
            partner[rows_of(c, y), :] = near[c]

        last_copy(c).start()
        return carry

    lax.fori_loop(0, chunks, forward, 0)
    finish_halo(lab_copies, lat, size)
    finish_halo(ana_copies, lat, size)

    def weigh(row, counts):
        here = labels[plane(sub, HALO + row), :]
        before = labels[plane(sub, HALO + row - 1), :]
        after = labels[plane(sub, HALO + row + 1), :]
        new = []
        for k in range(REGIONS):
            kept = jnp.where(here == k, 1.0, 0.0)
            around = jnp.where(before == k, 0.125, 0.0) + jnp.where(after == k, 0.125, 0.0)
            weights[k, plane(sub, row), :] = 0.25 * kept + around
            new.append(counts[k] + fold(kept))
        return new

    counts = lax.fori_loop(0, local_rows, weigh, [jnp.zeros((8, TILE), jnp.float32) for _ in range(REGIONS)])
    for k in range(REGIONS):
        tally[k : k + 1, :] = jnp.sum(counts[k], axis=0, keepdims=True)

    def finish(c, carry):
        near_copy(c).wait_send()
        last_copy(c).wait()
        return carry

    lax.fori_loop(0, chunks, finish, 0)


def rescale_kernel(
    size, local_rows, sub, first_ref, partner_ref, ana_ref, labels, weights, tally, state, factor_ref,
    spread, sums, send_sem, recv_sem, sum_send, sum_recv,
):
    lat = lax.axis_index("lat")
    mem = lax.axis_index("mem")
    extent = local_rows + 2 * HALO
    barrier = pltpu.get_barrier_semaphore()
    for hop in range(1, size):
        pl.semaphore_signal(barrier, inc=1, device_id=(mem, lax.rem(lat + hop, size)), device_id_type=MESH)
    clear_outside(spread, local_rows, sub, lat, size)

    def accumulate(row, energies):
        total = jnp.zeros((sub, TILE), jnp.float32)
        for field in range(FIELDS):
            there = plane(sub, field * local_rows + row)
            value = 0.5 * (first_ref[there, :] - partner_ref[there, :])
            spread[plane(sub, field * extent + HALO + row), :] = value
            total = total + value * value
        return [energies[k] + fold(total * weights[k, plane(sub, row), :]) for k in range(REGIONS)]

    energies = [jnp.zeros((8, TILE), jnp.float32) for _ in range(REGIONS)]
    energies = lax.fori_loop(0, local_rows, accumulate, energies, unroll=2)
    pl.semaphore_wait(barrier, size - 1)
    for k in range(REGIONS):
        sums[0, k : k + 1, :] = jnp.sum(energies[k], axis=0, keepdims=True)
    sums[0, REGIONS : 2 * REGIONS, :] = tally[...]
    shares = [
        pltpu.make_async_remote_copy(
            src_ref=sums.at[0],
            dst_ref=sums.at[hop],
            send_sem=sum_send.at[hop],
            recv_sem=sum_recv.at[hop],
            device_id=(mem, lax.rem(lat + hop, size)),
            device_id_type=MESH,
        )
        for hop in range(1, size)
    ]
    for copy in shares:
        copy.start()
    copies = halo_copies(spread, local_rows, sub, lat, size, send_sem, recv_sem)
    start_halo(copies, lat, size)
    for copy in shares:
        copy.wait()
    total = sums[0]
    for hop in range(1, size):
        total = total + sums[hop]
    total = jnp.sum(total, axis=1, keepdims=True)
    factor = target_size / jnp.sqrt(total[:REGIONS] / total[REGIONS:] + small_eps)
    wide = jnp.broadcast_to(factor, (REGIONS, TILE))
    diagonal = lax.broadcasted_iota(jnp.int32, (REGIONS, TILE), 0) == lax.broadcasted_iota(
        jnp.int32, (REGIONS, TILE), 1
    )
    factor_ref[...] = jnp.sum(jnp.where(diagonal, wide, 0.0), axis=0, keepdims=True)[:, :REGIONS]
    lanes = [jnp.broadcast_to(wide[k : k + 1], (sub, TILE)) for k in range(REGIONS)]

    def middle(e, carry):
        here = labels[plane(sub, e), :]
        scale = lanes[0]
        for k in range(1, REGIONS):
            scale = jnp.where(here == k, lanes[k], scale)
        for field in range(FIELDS):
            place = plane(sub, field * extent + e)
            state[place, :] = ana_ref[place, :] + scale * spread[place, :]
        return carry

    lax.fori_loop(HALO, HALO + local_rows, middle, 0, unroll=2)
    finish_halo(copies, lat, size)
    lax.fori_loop(0, HALO, middle, 0, unroll=2)
    lax.fori_loop(HALO + local_rows, extent, middle, 0, unroll=2)


def pair_call(tables, index, size, fields, local_rows, width):
    sub = width // TILE
    half = local_rows // COLUMNS
    chunks = fields * CHUNKS
    block = half // CHUNKS * sub
    extent = local_rows + 2 * HALO
    f32 = jnp.float32
    vmem = lambda *shape: pltpu.VMEM(shape, f32)
    pair = lambda *shape: [pltpu.SemaphoreType.DMA(shape)] * 2
    whole = pl.BlockSpec(memory_space=pltpu.VMEM)
    return pl.pallas_call(
        functools.partial(pair_kernel, tables, size, local_rows, sub),
        out_shape=(
            jax.ShapeDtypeStruct((fields * local_rows * sub, TILE), f32),
            jax.ShapeDtypeStruct((fields * extent * sub, TILE), f32),
            jax.ShapeDtypeStruct((extent * sub, TILE), f32),
            jax.ShapeDtypeStruct((REGIONS, local_rows * sub, TILE), f32),
            jax.ShapeDtypeStruct((REGIONS, TILE), f32),
        ),
        in_specs=[whole, pl.BlockSpec(memory_space=pltpu.HBM), whole, pl.BlockSpec(memory_space=pltpu.SMEM)],
        out_specs=(whole,) * 5,
        scratch_shapes=[
            vmem(fields, local_rows, width),
            vmem(chunks, block, TILE),
            vmem(2, chunks, block, TILE),
            vmem(2, chunks, block, TILE),
            vmem(chunks, block, TILE),
            pltpu.SemaphoreType.DMA((1,)),
        ]
        + pair(chunks)
        + pair(2, chunks)
        + pair(chunks)
        + pair(2, fields)
        + pair(2),
        compiler_params=pltpu.CompilerParams(
            collective_id=CLASS_ID + index, has_side_effects=True, vmem_limit_bytes=PAIR_VMEM
        ),
    )


def cycle(replica_variables, analysis, labels, pairing):
    size = lax.axis_size("lat")
    members = lax.axis_size("mem")
    fields, local_rows, width = analysis.shape
    sub = width // TILE
    extent = local_rows + 2 * HALO
    extended = jax.ShapeDtypeStruct((fields * extent * sub, TILE), jnp.float32)
    inner = jax.ShapeDtypeStruct((fields * local_rows * sub, TILE), jnp.float32)
    factors = jax.ShapeDtypeStruct((1, REGIONS), jnp.float32)
    patterns = level_patterns(members)
    whole = pl.BlockSpec(memory_space=pltpu.VMEM)
    smem = pl.BlockSpec(memory_space=pltpu.SMEM)
    halo_sems = [pltpu.SemaphoreType.DMA((2, fields)), pltpu.SemaphoreType.DMA((2, fields))]
    buffers = [
        pltpu.VMEM((fields * extent * sub, TILE), jnp.float32),
        pltpu.VMEM((extent * sub, TILE), jnp.float32),
    ]
    state = pl.pallas_call(
        functools.partial(opening_kernel, size, local_rows, sub),
        out_shape=extended,
        in_specs=[pl.BlockSpec(memory_space=pltpu.HBM)],
        out_specs=whole,
        scratch_shapes=[pltpu.VMEM(analysis.shape, jnp.float32), pltpu.SemaphoreType.DMA((fields,))] + halo_sems,
        compiler_params=pltpu.CompilerParams(collective_id=0, has_side_effects=True, vmem_limit_bytes=OPEN_VMEM),
    )(replica_variables[0])
    first, index = pl.pallas_call(
        functools.partial(first_steps_kernel, size, local_rows, sub, patterns),
        out_shape=(inner, jax.ShapeDtypeStruct((1, 1), jnp.int32)),
        in_specs=[whole, smem],
        out_specs=(whole, smem),
        scratch_shapes=buffers,
        compiler_params=pltpu.CompilerParams(vmem_limit_bytes=PAIR_VMEM),
    )(state, pairing)
    branches = [
        pair_call(slot_tables(edges, members // COLUMNS), k, size, fields, local_rows, width)
        for k, edges in enumerate(patterns)
    ]
    partner, ana, label_planes, weights, tally = lax.switch(index[0, 0], branches, first, analysis, labels, pairing)
    state, factor = pl.pallas_call(
        functools.partial(rescale_kernel, size, local_rows, sub),
        out_shape=(extended, factors),
        in_specs=[whole] * 6,
        out_specs=(whole, whole),
        scratch_shapes=[
            pltpu.VMEM((fields * extent * sub, TILE), jnp.float32),
            pltpu.VMEM((size, 2 * REGIONS, TILE), jnp.float32),
        ]
        + halo_sems
        + [pltpu.SemaphoreType.DMA((size,)), pltpu.SemaphoreType.DMA((size,))],
        compiler_params=pltpu.CompilerParams(collective_id=1, has_side_effects=True, vmem_limit_bytes=PAIR_VMEM),
    )(first, partner, ana, label_planes, weights, tally)
    closing, factor = pl.pallas_call(
        functools.partial(steps_kernel, size, local_rows, sub, True),
        out_shape=(jax.ShapeDtypeStruct(analysis.shape, jnp.float32), factors),
        in_specs=[whole] * 2,
        out_specs=(whole, whole),
        scratch_shapes=buffers,
        compiler_params=pltpu.CompilerParams(vmem_limit_bytes=VMEM_LIMIT),
    )(state, factor)
    return (closing[None], factor)


def either(replica_variables, analysis, labels, pairing):
    members, rows = lax.axis_size("mem"), analysis.shape[1]
    levels = members // COLUMNS
    fits = members % COLUMNS == 0 and 2 <= levels <= MAX_LEVELS
    if fits and rows == 8 * COLUMNS and rows % (FIELDS * CHUNKS) == 0 and lax.axis_size("lat") > 1:
        return cycle(replica_variables, analysis, labels, pairing)
    return local(replica_variables, analysis, labels, pairing)


def solution(mesh):
    return jax.shard_map(
        either,
        mesh=mesh,
        in_specs=(P("mem", None, "lat", None), P(None, "lat", None), P("lat", None), P()),
        out_specs=(P("mem", None, "lat", None), P("mem", None)),
        check_vma=False,
    )
```

```python
import functools

import jax
import jax.numpy as jnp
from jax import lax
from jax.experimental import pallas as pl
from jax.experimental.pallas import tpu as pltpu
from jax.sharding import PartitionSpec as P

MESH = pl.DeviceIdType.MESH
TILE = 128
REGIONS = 8
STEPS = 3
MAX_BRANCHES = 28
MAX_LEVELS = 4
OPEN_VMEM = 8 * 2**20
HALO = 2 * STEPS
VMEM_LIMIT = 24 * 2**20
FIELDS = 4
REACH = (2 * STEPS - 1, 2 * STEPS - 1, 2 * STEPS, STEPS)


grav_coef = 0.1
depth_coef = 0.1
advect_coef = 0.05
diffuse_coef = 0.05
coriolis_coef = 0.05
target_size = 0.5
small_eps = 1e-06


def shift_lon(plane):
    sub = plane.shape[0]
    lane = lax.broadcasted_iota(jnp.int32, plane.shape, 1)
    east = pltpu.roll(plane, TILE - 1, 1)
    east = jnp.where(lane == TILE - 1, pltpu.roll(east, sub - 1, 0), east)
    west = pltpu.roll(plane, 1, 1)
    west = jnp.where(lane == 0, pltpu.roll(west, 1, 0), west)
    return east, west


def diff_lon(plane):
    east, west = shift_lon(plane)
    return east - west


def run_steps(state, buf, spare, local_rows, sub, start, rows_all):
    extent = local_rows + 2 * HALO

    def at(field, e):
        return pl.ds((field * extent + e) * sub, sub)

    def masked(e, plane):
        if HALO <= e < HALO + local_rows:
            return plane
        row = start + (e - HALO)
        return jnp.where((row >= 0) & (row < rows_all), 1.0, 0.0).astype(jnp.float32) * plane

    def coriolis(e):
        row = (start + (e - HALO)).astype(jnp.float32)
        return coriolis_coef * (2.0 * (row + 0.5) / rows_all - 1.0)

    tracer_source, source_field = state, 3
    for step in range(STEPS):
        margin = 2 * (STEPS - 1 - step)
        narrow = STEPS - 1 - step
        target, target_field = (spare, 0) if step % 2 == 0 else (buf, 3)
        own = (HALO, HALO + local_rows)
        for e in range(own[0] - margin - 1, own[1] + margin + 1):
            divergence = diff_lon(state[at(1, e), :]) + state[at(2, e + 1), :] - state[at(2, e - 1), :]
            buf[at(0, e), :] = masked(e, state[at(0, e), :] - depth_coef * divergence)
        for e in range(own[0] - margin, own[1] + margin):
            f = coriolis(e)
            v = state[at(2, e), :]
            u1 = state[at(1, e), :] + f * v - grav_coef * diff_lon(buf[at(0, e), :])
            slope = buf[at(0, e + 1), :] - buf[at(0, e - 1), :]
            buf[at(1, e), :] = u1
            buf[at(2, e), :] = masked(e, v - f * u1 - grav_coef * slope)
        for e in range(own[0] - narrow, own[1] + narrow):
            q = tracer_source[at(source_field, e), :]
            upper = tracer_source[at(source_field, e + 1), :]
            lower = tracer_source[at(source_field, e - 1), :]
            east, west = shift_lon(q)
            advected = buf[at(1, e), :] * (east - west) + buf[at(2, e), :] * (upper - lower)
            spreading = east + west + upper + lower - 4.0 * q
            target[at(target_field, e), :] = masked(e, q - advect_coef * advected + diffuse_coef * spreading)
        state = buf
        tracer_source, source_field = target, target_field
    return [(buf, 0), (buf, 1), (buf, 2), (tracer_source, source_field)]


def pairs_of(size):
    return [(a, b) for a in range(size) for b in range(a + 1, size)]


def pair_index(pairing_ref):
    size = pairing_ref.shape[0]
    me = lax.axis_index("mem")
    partner = pairing_ref[me]
    low, high = jnp.minimum(me, partner), jnp.maximum(me, partner)
    return low * (2 * size - low - 1) // 2 + high - low - 1


def steps_kernel(size, local_rows, sub, as_rows, *refs):
    extent = local_rows + 2 * HALO
    if as_rows:
        state_ref, factor_ref, out_ref, factor_out, buf, spare = refs
        factor_out[...] = factor_ref[...]
    else:
        state_ref, pairing_ref, out_ref, index_ref, buf, spare = refs
        index_ref[0, 0] = pair_index(pairing_ref)
    lat = lax.axis_index("lat")
    fields = run_steps(state_ref, buf, spare, local_rows, sub, lat * local_rows, local_rows * size)
    for field, (ref, place) in enumerate(fields):
        if not as_rows:
            for tile in range(local_rows * sub // 8):
                column = (field * local_rows * sub // 8 + tile) * TILE
                out_ref[:, column : column + TILE] = ref[pl.ds((place * extent + HALO) * sub + tile * 8, 8), :]
            continue
        for row in range(0, local_rows, 8):
            for t in range(sub):
                first = (place * extent + HALO + row) * sub + t
                out_ref[field, row : row + 8, t * TILE : (t + 1) * TILE] = ref[pl.ds(first, 8, stride=sub), :]


def halo_copies(buf, local_rows, sub, lat, size, send_sem, recv_sem):
    extent = local_rows + 2 * HALO
    mem = lax.axis_index("mem")
    copies = []
    for side, peer in ((0, lat - 1), (1, lat + 1)):
        group = []
        for field in range(FIELDS):
            reach = REACH[field]
            source = HALO if side == 0 else HALO + local_rows - reach
            target = HALO + local_rows if side == 0 else HALO - reach
            group.append(
                pltpu.make_async_remote_copy(
                    src_ref=buf.at[pl.ds((field * extent + source) * sub, reach * sub), :],
                    dst_ref=buf.at[pl.ds((field * extent + target) * sub, reach * sub), :],
                    send_sem=send_sem.at[side, field],
                    recv_sem=recv_sem.at[side, field],
                    device_id=(mem, peer),
                    device_id_type=MESH,
                )
            )
        copies.append(group)
    return copies


def clear_outside(buf, local_rows, sub, lat, size):
    extent = local_rows + 2 * HALO
    zeros = jnp.zeros((HALO * sub, TILE), jnp.float32)

    @pl.when(lat == 0)
    def _():
        for field in range(FIELDS):
            buf[pl.ds(field * extent * sub, HALO * sub), :] = zeros

    @pl.when(lat == size - 1)
    def _():
        for field in range(FIELDS):
            buf[pl.ds((field * extent + HALO + local_rows) * sub, HALO * sub), :] = zeros


def start_halo(copies, lat, size):
    for side, has in ((0, lat > 0), (1, lat < size - 1)):

        @pl.when(has)
        def _(side=side):
            for copy in copies[side]:
                copy.start()


def finish_halo(copies, lat, size):
    for side, has in ((0, lat > 0), (1, lat < size - 1)):

        @pl.when(has)
        def _(side=side):
            for copy in copies[side]:
                copy.wait_send()
            for copy in copies[1 - side]:
                copy.wait_recv()


def planes_from_rows(source, buf, local_rows, sub, fields=range(FIELDS)):
    extent = local_rows + 2 * HALO
    for field in fields:
        for row in range(0, local_rows, 8):
            for t in range(sub):
                first = (field * extent + HALO + row) * sub + t
                buf[pl.ds(first, 8, stride=sub), :] = source[field, row : row + 8, t * TILE : (t + 1) * TILE]


def first_kernel(size, local_rows, sub, x_ref, lab_ref, buf, edge_ref, rows, load_sem, send_sem, recv_sem, lab_send, lab_recv):
    lat = lax.axis_index("lat")
    mem = lax.axis_index("mem")
    barrier = pltpu.get_barrier_semaphore()
    for peer, has in ((lat - 1, lat > 0), (lat + 1, lat < size - 1)):

        @pl.when(has)
        def _(peer=peer):
            pl.semaphore_signal(barrier, inc=1, device_id=(mem, peer), device_id_type=MESH)

    loads = [pltpu.make_async_copy(x_ref.at[f], rows.at[f], load_sem.at[f]) for f in range(FIELDS)]
    for load in loads:
        load.start()
    clear_outside(buf, local_rows, sub, lat, size)
    none = jnp.full((sub, TILE), -1.0, jnp.float32)

    @pl.when(lat == 0)
    def _():
        edge_ref[0] = none

    @pl.when(lat == size - 1)
    def _():
        edge_ref[1] = none

    inner = (lat > 0) & (lat < size - 1)

    @pl.when(inner)
    def _():
        pl.semaphore_wait(barrier, 2)

    @pl.when(jnp.logical_not(inner))
    def _():
        pl.semaphore_wait(barrier, 1)

    copies = halo_copies(buf, local_rows, sub, lat, size, send_sem, recv_sem)
    for side, peer in ((0, lat - 1), (1, lat + 1)):
        row = 0 if side == 0 else local_rows - 1
        copies[side].append(
            pltpu.make_async_remote_copy(
                src_ref=lab_ref.at[row],
                dst_ref=edge_ref.at[1 - side],
                send_sem=lab_send.at[side],
                recv_sem=lab_recv.at[side],
                device_id=(mem, peer),
                device_id_type=MESH,
            )
        )
    for field in range(FIELDS + 1):
        if field < FIELDS:
            loads[field].wait()
            planes_from_rows(rows, buf, local_rows, sub, (field,))
        start_halo([side[field : field + 1] for side in copies], lat, size)
    finish_halo(copies, lat, size)


def second_kernel(
    size, local_rows, sub, first_ref, partner_ref, analysis_ref, lab_ref, edge_ref, buf, factor_ref,
    spread, sums, send_sem, recv_sem, sum_send, sum_recv,
):
    lat = lax.axis_index("lat")
    mem = lax.axis_index("mem")
    extent = local_rows + 2 * HALO
    barrier = pltpu.get_barrier_semaphore()
    for hop in range(1, size):
        pl.semaphore_signal(barrier, inc=1, device_id=(mem, lax.rem(lat + hop, size)), device_id_type=MESH)

    def fold(plane):
        total = plane[0:8]
        for i in range(8, sub, 8):
            total = total + plane[i : i + 8]
        return total

    energies = [jnp.zeros((8, TILE), jnp.float32) for _ in range(REGIONS)]
    counts = [jnp.zeros((8, TILE), jnp.float32) for _ in range(REGIONS)]

    def accumulate(row, carry):
        energies, counts = carry
        total = jnp.zeros((sub, TILE), jnp.float32)
        for field in range(FIELDS):
            parts = []
            for i in range(sub // 8):
                column = ((field * local_rows + row) * (sub // 8) + i) * TILE
                place = pl.ds(pl.multiple_of(column, TILE), TILE)
                parts.append(first_ref[:, place] - partner_ref[:, place])
            half = 0.5 * jnp.concatenate(parts, axis=0)
            spread[field, row] = half
            total = total + half * half
        quarter = 0.125 * total
        here = lab_ref[row]
        before = jnp.where(row == 0, edge_ref[0], lab_ref[jnp.maximum(row - 1, 0)])
        after = jnp.where(row == local_rows - 1, edge_ref[1], lab_ref[jnp.minimum(row + 1, local_rows - 1)])
        new_energies, new_counts = [], []
        for k in range(REGIONS):
            kept = jnp.where(here == k, 1.0, 0.0)
            weight = 2.0 * kept + jnp.where(before == k, 1.0, 0.0) + jnp.where(after == k, 1.0, 0.0)
            new_energies.append(energies[k] + fold(quarter * weight))
            new_counts.append(counts[k] + fold(kept))
        return new_energies, new_counts

    energies, counts = lax.fori_loop(0, local_rows, accumulate, (energies, counts))
    for k in range(REGIONS):
        sums[0, k : k + 1, :] = jnp.sum(energies[k], axis=0, keepdims=True)
        sums[0, REGIONS + k : REGIONS + k + 1, :] = jnp.sum(counts[k], axis=0, keepdims=True)

    pl.semaphore_wait(barrier, size - 1)
    sends = []
    for hop in range(1, size):
        sends.append(
            pltpu.make_async_remote_copy(
                src_ref=sums.at[0],
                dst_ref=sums.at[hop],
                send_sem=sum_send.at[hop],
                recv_sem=sum_recv.at[hop],
                device_id=(mem, lax.rem(lat + hop, size)),
                device_id_type=MESH,
            )
        )
    for copy in sends:
        copy.start()
    clear_outside(buf, local_rows, sub, lat, size)
    planes_from_rows(analysis_ref, buf, local_rows, sub)
    for copy in sends:
        copy.wait()
    total = sums[0]
    for hop in range(1, size):
        total = total + sums[hop]
    total = jnp.sum(total, axis=1, keepdims=True)
    factor = target_size / jnp.sqrt(total[:REGIONS] / total[REGIONS:] + small_eps)
    wide = jnp.broadcast_to(factor, (REGIONS, TILE))
    diagonal = lax.broadcasted_iota(jnp.int32, (REGIONS, TILE), 0) == lax.broadcasted_iota(
        jnp.int32, (REGIONS, TILE), 1
    )
    factor_ref[...] = jnp.sum(jnp.where(diagonal, wide, 0.0), axis=0, keepdims=True)[:, :REGIONS]
    lanes = [jnp.broadcast_to(wide[k : k + 1], (sub, TILE)) for k in range(REGIONS)]

    def middle(row, carry):
        here = lab_ref[row]
        scale = lanes[0]
        for k in range(1, REGIONS):
            scale = jnp.where(here == k, lanes[k], scale)
        for field in range(FIELDS):
            place = pl.ds(pl.multiple_of((field * extent + HALO + row) * sub, sub), sub)
            buf[place, :] = buf[place, :] + scale * spread[field, row]
        return carry

    lax.fori_loop(0, local_rows, middle, 0)
    copies = halo_copies(buf, local_rows, sub, lat, size, send_sem, recv_sem)
    start_halo(copies, lat, size)
    finish_halo(copies, lat, size)


def partner_fields(fields, pairing, index):
    pairs = pairs_of(lax.axis_size("mem"))
    if len(pairs) > MAX_BRANCHES:
        piece = lax.all_gather(fields, "mem", axis=0)
        return lax.dynamic_index_in_dim(piece, pairing[lax.axis_index("mem")], 0, keepdims=False)
    branches = [
        functools.partial(lax.ppermute, axis_name="mem", perm=[(a, b), (b, a)]) for a, b in pairs
    ]
    return lax.switch(index, branches, fields)


def local(replica_variables, analysis, labels, pairing):
    size = lax.axis_size("lat")
    fields, local_rows, width = analysis.shape
    sub = width // TILE
    extent = local_rows + 2 * HALO
    wide = jax.ShapeDtypeStruct((8, fields * local_rows * width // 8), jnp.float32)
    extended = jax.ShapeDtypeStruct((fields * extent * sub, TILE), jnp.float32)
    edges = jax.ShapeDtypeStruct((2, sub, TILE), jnp.float32)
    factors = jax.ShapeDtypeStruct((1, REGIONS), jnp.float32)
    label_planes = jnp.broadcast_to(labels.astype(jnp.float32)[..., None], (local_rows, sub, TILE))
    whole = pl.BlockSpec(memory_space=pltpu.VMEM)
    buffers = [
        pltpu.VMEM((fields * extent * sub, TILE), jnp.float32),
        pltpu.VMEM((extent * sub, TILE), jnp.float32),
    ]
    halo_sems = [pltpu.SemaphoreType.DMA((2, fields)), pltpu.SemaphoreType.DMA((2, fields))]
    state, edge = pl.pallas_call(
        functools.partial(first_kernel, size, local_rows, sub),
        out_shape=(extended, edges),
        in_specs=[pl.BlockSpec(memory_space=pltpu.HBM), whole],
        out_specs=(whole, whole),
        scratch_shapes=[pltpu.VMEM(analysis.shape, jnp.float32), pltpu.SemaphoreType.DMA((fields,))]
        + halo_sems
        + [pltpu.SemaphoreType.DMA((2,)), pltpu.SemaphoreType.DMA((2,))],
        compiler_params=pltpu.CompilerParams(collective_id=0, has_side_effects=True, vmem_limit_bytes=VMEM_LIMIT),
    )(replica_variables[0], label_planes)
    smem = pl.BlockSpec(memory_space=pltpu.SMEM)
    first, index = pl.pallas_call(
        functools.partial(steps_kernel, size, local_rows, sub, False),
        out_shape=(wide, jax.ShapeDtypeStruct((1, 1), jnp.int32)),
        in_specs=[whole, smem],
        out_specs=(whole, smem),
        scratch_shapes=buffers,
        compiler_params=pltpu.CompilerParams(vmem_limit_bytes=VMEM_LIMIT),
    )(state, pairing)
    partner = partner_fields(first, pairing, index[0, 0])
    state, factor = pl.pallas_call(
        functools.partial(second_kernel, size, local_rows, sub),
        out_shape=(extended, factors),
        in_specs=[whole] * 5,
        out_specs=(whole, whole),
        scratch_shapes=[
            pltpu.VMEM((fields, local_rows, sub, TILE), jnp.float32),
            pltpu.VMEM((size, 2 * REGIONS, TILE), jnp.float32),
        ]
        + halo_sems
        + [pltpu.SemaphoreType.DMA((size,)), pltpu.SemaphoreType.DMA((size,))],
        compiler_params=pltpu.CompilerParams(collective_id=1, has_side_effects=True, vmem_limit_bytes=VMEM_LIMIT),
    )(first, partner, analysis, label_planes, edge)
    closing, factor = pl.pallas_call(
        functools.partial(steps_kernel, size, local_rows, sub, True),
        out_shape=(jax.ShapeDtypeStruct(analysis.shape, jnp.float32), factors),
        in_specs=[whole] * 2,
        out_specs=(whole, whole),
        scratch_shapes=buffers,
        compiler_params=pltpu.CompilerParams(vmem_limit_bytes=VMEM_LIMIT),
    )(state, factor)
    return (closing[None], factor)


CLASS_ID = 2
COLUMNS = 2
CHUNKS = 2
PAIR_VMEM = 16 * 2**20


def matchings(items):
    if not items:
        return [()]
    head, found = items[0], []
    for i in range(1, len(items)):
        for rest in matchings(items[1:i] + items[i + 1 :]):
            found.append(((head, items[i]),) + rest)
    return found


def level_edges(matching):
    return tuple(sorted(tuple(sorted((a // COLUMNS, b // COLUMNS))) for a, b in matching))


def level_patterns(size):
    return sorted({level_edges(m) for m in matchings(tuple(range(size)))})


def slot_tables(edges, levels):
    peer = [[z, z] for z in range(levels)]
    slot = [[0, 1] for _ in range(levels)]
    moves = [0] * levels
    used = [0] * levels
    for a, b in edges:
        if a == b:
            continue
        i, j = used[a], used[b]
        used[a] += 1
        used[b] += 1
        peer[a][i], slot[a][i] = b, j
        peer[b][j], slot[b][j] = a, i
        moves[a] = moves[b] = 1
    return peer, slot, moves


def pattern_index(patterns, pairing_ref):
    members = pairing_ref.shape[0]
    levels = members // COLUMNS
    level = [lax.div(pairing_ref[m], COLUMNS) for m in range(members)]
    count = {}
    for a in range(levels):
        for b in range(a + 1, levels):
            count[a, b] = sum(jnp.where(level[a * COLUMNS + i] == b, 1, 0) for i in range(COLUMNS))
    index = jnp.int32(0)
    for k, edges in enumerate(patterns):
        good = None
        for pair, n in count.items():
            same = n == sum(e == pair for e in edges)
            good = same if good is None else good & same
        index = jnp.where(good, k, index)
    return index


def lookup(index, table):
    value = jnp.int32(table[0])
    for k, entry in enumerate(table):
        if k and entry != table[0]:
            value = jnp.where(index == k, entry, value)
    return value


def opening_kernel(size, local_rows, sub, x_ref, buf, rows, load_sem, send_sem, recv_sem):
    lat = lax.axis_index("lat")
    mem = lax.axis_index("mem")
    barrier = pltpu.get_barrier_semaphore()
    for peer, has in ((lat - 1, lat > 0), (lat + 1, lat < size - 1)):

        @pl.when(has)
        def _(peer=peer):
            pl.semaphore_signal(barrier, inc=1, device_id=(mem, peer), device_id_type=MESH)

    loads = [pltpu.make_async_copy(x_ref.at[f], rows.at[f], load_sem.at[f]) for f in range(FIELDS)]
    for load in loads:
        load.start()
    clear_outside(buf, local_rows, sub, lat, size)
    inner = (lat > 0) & (lat < size - 1)

    @pl.when(inner)
    def _():
        pl.semaphore_wait(barrier, 2)

    @pl.when(jnp.logical_not(inner))
    def _():
        pl.semaphore_wait(barrier, 1)

    copies = halo_copies(buf, local_rows, sub, lat, size, send_sem, recv_sem)
    for field in range(FIELDS):
        loads[field].wait()
        planes_from_rows(rows, buf, local_rows, sub, (field,))
        start_halo([side[field : field + 1] for side in copies], lat, size)
    finish_halo(copies, lat, size)


def first_steps_kernel(size, local_rows, sub, patterns, state_ref, pairing_ref, out_ref, index_ref, buf, spare):
    extent = local_rows + 2 * HALO
    index_ref[0, 0] = pattern_index(patterns, pairing_ref)
    lat = lax.axis_index("lat")
    fields = run_steps(state_ref, buf, spare, local_rows, sub, lat * local_rows, local_rows * size)
    for field, (ref, place) in enumerate(fields):
        for tile in range(local_rows * sub // 8):
            out_ref[pl.ds((field * local_rows * sub) + tile * 8, 8), :] = ref[
                pl.ds((place * extent + HALO) * sub + tile * 8, 8), :
            ]


def plane(sub, index):
    return pl.ds(pl.multiple_of(index * sub, sub), sub)


def fold(block):
    total = block[0:8]
    for i in range(8, block.shape[0], 8):
        total = total + block[i : i + 8]
    return total


def pair_kernel(
    tables, size, local_rows, sub,
    first_ref, analysis_ref, lab_ref, pairing_ref,
    state, factor_ref,
    av, near, send, came, onward, final, spread, labels, weights, energy, tally, sums,
    load_sem, near_send, near_recv, z_send, z_recv, last_send, last_recv,
    ana_send, ana_recv, lab_send, lab_recv, halo_send, halo_recv, sum_send, sum_recv,
):
    lat = lax.axis_index("lat")
    mem = lax.axis_index("mem")
    z, y = lax.div(mem, COLUMNS), lax.rem(mem, COLUMNS)
    peer_table, slot_table, moves_table = tables
    levels = len(moves_table)
    half = local_rows // COLUMNS
    deep = half // CHUNKS
    block = deep * sub
    chunks = FIELDS * CHUNKS
    extent = local_rows + 2 * HALO
    other = (z * COLUMNS + 1 - y, lat)
    peers = [lookup(z, [peer_table[k][j] for k in range(levels)]) for j in range(2)]
    slots = [lookup(z, [slot_table[k][j] for k in range(levels)]) for j in range(2)]
    moves = lookup(z, moves_table) == 1

    load = pltpu.make_async_copy(analysis_ref, av, load_sem.at[0])
    load.start()
    barrier = pltpu.get_barrier_semaphore()
    pl.semaphore_signal(barrier, inc=1, device_id=other, device_id_type=MESH)

    @pl.when(moves)
    def _():
        for j in range(2):
            pl.semaphore_signal(barrier, inc=1, device_id=(peers[j] * COLUMNS + y, lat), device_id_type=MESH)

    for hop in range(1, size):
        pl.semaphore_signal(barrier, inc=1, device_id=(mem, lax.rem(lat + hop, size)), device_id_type=MESH)
    clear_outside(state, local_rows, sub, lat, size)
    clear_outside(spread, local_rows, sub, lat, size)
    none = jnp.full((HALO * sub, TILE), -1.0, jnp.float32)

    @pl.when(lat == 0)
    def _():
        labels[pl.ds(0, HALO * sub), :] = none

    @pl.when(lat == size - 1)
    def _():
        labels[pl.ds((HALO + local_rows) * sub, HALO * sub), :] = none

    @pl.when(moves)
    def _():
        pl.semaphore_wait(barrier, size + 2)

    @pl.when(jnp.logical_not(moves))
    def _():
        pl.semaphore_wait(barrier, size)

    def rows_of(c, column):
        field, part = lax.div(c, CHUNKS), lax.rem(c, CHUNKS)
        return pl.ds(pl.multiple_of((field * local_rows + column * half + part * deep) * sub, sub), block)

    def near_copy(c):
        return pltpu.make_async_remote_copy(
            src_ref=first_ref.at[rows_of(c, 1 - y), :],
            dst_ref=near.at[c],
            send_sem=near_send.at[c],
            recv_sem=near_recv.at[c],
            device_id=other,
            device_id_type=MESH,
        )

    def cross_copy(c, j, slot):
        return pltpu.make_async_remote_copy(
            src_ref=send.at[j, c],
            dst_ref=came.at[slot, c],
            send_sem=z_send.at[j, c],
            recv_sem=z_recv.at[slot, c],
            device_id=(peers[j] * COLUMNS + y, lat),
            device_id_type=MESH,
        )

    def last_copy(c):
        return pltpu.make_async_remote_copy(
            src_ref=onward.at[c],
            dst_ref=final.at[c],
            send_sem=last_send.at[c],
            recv_sem=last_recv.at[c],
            device_id=other,
            device_id_type=MESH,
        )

    def halo_copy(field, reach, side, peer):
        source = HALO if side == 0 else HALO + local_rows - reach
        target = HALO + local_rows if side == 0 else HALO - reach
        return pltpu.make_async_remote_copy(
            src_ref=spread.at[pl.ds(pl.multiple_of((field * extent + source) * sub, sub), reach * sub), :],
            dst_ref=spread.at[pl.ds(pl.multiple_of((field * extent + target) * sub, sub), reach * sub), :],
            send_sem=halo_send.at[side, field],
            recv_sem=halo_recv.at[side, field],
            device_id=(mem, peer),
            device_id_type=MESH,
        )

    def start_near(c, carry):
        near_copy(c).start()
        return carry

    lax.fori_loop(0, chunks, start_near, 0)

    pick = [pairing_ref[z * COLUMNS + i] for i in range(COLUMNS)]
    pick_level = [lax.div(p, COLUMNS) for p in pick]
    first_slot_item = jnp.where(pick_level[0] == peers[0], 0, 1)
    here_level = jnp.where(y == 0, pick_level[0], pick_level[1])
    here_column = lax.rem(jnp.where(y == 0, pick[0], pick[1]), COLUMNS)
    keep_slot = jnp.where(peers[0] == peers[1], here_column, jnp.where(here_level == peers[0], 0, 1))
    own_first = jnp.full((sub, TILE), first_slot_item, jnp.int32) == y
    keep_first = jnp.full((sub, TILE), keep_slot, jnp.int32) == 0
    diagonal = lax.broadcasted_iota(jnp.int32, (sub, sub), 0) == lax.broadcasted_iota(jnp.int32, (sub, sub), 1)

    def label_row(row, carry):
        line = jnp.broadcast_to(lab_ref[pl.ds(row, 1), :].astype(jnp.float32), (sub, sub))
        column = jnp.sum(jnp.where(diagonal, line, 0.0), axis=1, keepdims=True)
        labels[plane(sub, HALO + row), :] = jnp.broadcast_to(column, (sub, TILE))
        return carry

    lax.fori_loop(0, local_rows, label_row, 0, unroll=4)
    lab_copies = [
        [
            pltpu.make_async_remote_copy(
                src_ref=labels.at[pl.ds(HALO * sub if side == 0 else local_rows * sub, HALO * sub), :],
                dst_ref=labels.at[pl.ds((HALO + local_rows) * sub if side == 0 else 0, HALO * sub), :],
                send_sem=lab_send.at[side],
                recv_sem=lab_recv.at[side],
                device_id=(mem, peer),
                device_id_type=MESH,
            )
        ]
        for side, peer in ((0, lat - 1), (1, lat + 1))
    ]
    start_halo(lab_copies, lat, size)
    load.wait()
    tiles = FIELDS * sub // chunks

    def lay_out(c):
        for i in range(tiles):
            index = c * tiles + i
            field, tile = lax.div(index, sub), lax.rem(index, sub)
            for row in range(0, local_rows, 8):
                state[pl.ds((field * extent + HALO + row) * sub + tile, 8, stride=sub), :] = av[
                    field, row : row + 8, pl.ds(pl.multiple_of(tile * TILE, TILE), TILE)
                ]

    def cross(c, carry):
        near_copy(c).wait_recv()

        @pl.when(moves)
        def _():
            start = rows_of(c, y).start
            for r in range(deep):
                here = pl.ds(r * sub, sub)
                a = first_ref[pl.ds(pl.multiple_of(start + r * sub, sub), sub), :]
                b = near[c, here, :]
                send[0, c, here, :] = jnp.where(own_first, a, b)
                send[1, c, here, :] = jnp.where(own_first, b, a)
            for j in range(2):
                cross_copy(c, j, slots[j]).start()

        lay_out(c)
        return carry

    lax.fori_loop(0, chunks, cross, 0)
    ana_copies = halo_copies(state, local_rows, sub, lat, size, ana_send, ana_recv)
    start_halo(ana_copies, lat, size)
    finish_halo(lab_copies, lat, size)

    def weigh(row, counts):
        here = labels[plane(sub, HALO + row), :]
        before = labels[plane(sub, HALO + row - 1), :]
        after = labels[plane(sub, HALO + row + 1), :]
        new = []
        for k in range(REGIONS):
            kept = jnp.where(here == k, 1.0, 0.0)
            around = jnp.where(before == k, 0.125, 0.0) + jnp.where(after == k, 0.125, 0.0)
            weights[k, plane(sub, row), :] = 0.25 * kept + around
            new.append(counts[k] + fold(kept))
        return new

    counts = lax.fori_loop(0, local_rows, weigh, [jnp.zeros((8, TILE), jnp.float32) for _ in range(REGIONS)])
    for k in range(REGIONS):
        tally[pl.ds(k * 8, 8), :] = counts[k]
    energy[...] = jnp.zeros_like(energy)

    def absorb(field, first_row, theirs):
        totals = [energy[pl.ds(k * 8, 8), :] for k in range(REGIONS)]
        for r in range(deep):
            row = first_row + r
            value = 0.5 * (first_ref[plane(sub, field * local_rows + row), :] - theirs[r * sub : (r + 1) * sub, :])
            spread[plane(sub, field * extent + HALO + row), :] = value
            square = value * value
            for k in range(REGIONS):
                totals[k] = totals[k] + fold(square * weights[k, plane(sub, row), :])
        for k in range(REGIONS):
            energy[pl.ds(k * 8, 8), :] = totals[k]

    def forward(field, part):
        c = field * CHUNKS + part

        @pl.when(moves)
        def _():
            for j in range(2):
                cross_copy(c, j, j).wait_recv()
            for r in range(deep):
                here = pl.ds(r * sub, sub)
                a = came[0, c, here, :]
                b = came[1, c, here, :]
                onward[c, here, :] = jnp.where(keep_first, b, a)
                near[c, here, :] = jnp.where(keep_first, a, b)

        @pl.when(jnp.logical_not(moves))
        def _():
            onward[c] = first_ref[rows_of(c, y), :]

        last_copy(c).start()

        absorb(field, y * half + part * deep, near.at[c])

    def arrive(field, part):
        c = field * CHUNKS + part
        last_copy(c).wait_recv()
        absorb(field, (1 - y) * half + part * deep, final.at[c])

    sides = ((0, lat - 1, lat > 0), (1, lat + 1, lat < size - 1))

    def send_halo(field, reach):
        for side, peer, has in sides:

            @pl.when(has)
            def _(side=side, peer=peer):
                halo_copy(field, reach, side, peer).start()

    def stage(c, carry):
        @pl.when(c < chunks)
        def _():
            forward(lax.div(c, CHUNKS), lax.rem(c, CHUNKS))

        @pl.when(c > 0)
        def _():
            field, part = lax.div(c - 1, CHUNKS), lax.rem(c - 1, CHUNKS)
            arrive(field, part)

            @pl.when((part == CHUNKS - 1) & (field < FIELDS - 1))
            def _():
                send_halo(field, HALO)

        return carry

    lax.fori_loop(0, chunks + 1, stage, 0)
    send_halo(FIELDS - 1, REACH[FIELDS - 1])
    for k in range(REGIONS):
        for i, table in enumerate((energy, tally)):
            sums[0, i * REGIONS + k : i * REGIONS + k + 1, :] = jnp.sum(
                table[pl.ds(k * 8, 8), :], axis=0, keepdims=True
            )
    shares = [
        pltpu.make_async_remote_copy(
            src_ref=sums.at[0],
            dst_ref=sums.at[hop],
            send_sem=sum_send.at[hop],
            recv_sem=sum_recv.at[hop],
            device_id=(mem, lax.rem(lat + hop, size)),
            device_id_type=MESH,
        )
        for hop in range(1, size)
    ]
    for copy in shares:
        copy.start()
    finish_halo(ana_copies, lat, size)

    def finish(c, carry):
        near_copy(c).wait_send()
        last_copy(c).wait_send()

        @pl.when(moves)
        def _():
            for j in range(2):
                cross_copy(c, j, j).wait_send()

        return carry

    lax.fori_loop(0, chunks, finish, 0)
    for copy in shares:
        copy.wait()
    total = sums[0]
    for hop in range(1, size):
        total = total + sums[hop]
    total = jnp.sum(total, axis=1, keepdims=True)
    factor = target_size / jnp.sqrt(total[:REGIONS] / total[REGIONS:] + small_eps)
    wide = jnp.broadcast_to(factor, (REGIONS, TILE))
    corner = lax.broadcasted_iota(jnp.int32, (REGIONS, TILE), 0) == lax.broadcasted_iota(
        jnp.int32, (REGIONS, TILE), 1
    )
    factor_ref[...] = jnp.sum(jnp.where(corner, wide, 0.0), axis=0, keepdims=True)[:, :REGIONS]
    lanes = [jnp.broadcast_to(wide[k : k + 1], (sub, TILE)) for k in range(REGIONS)]

    def middle(e, carry):
        here = labels[plane(sub, e), :]
        scale = lanes[0]
        for k in range(1, REGIONS):
            scale = jnp.where(here == k, lanes[k], scale)
        for field in range(FIELDS):
            place = plane(sub, field * extent + e)
            state[place, :] = state[place, :] + scale * spread[place, :]
        return carry

    for field in range(FIELDS):
        reach = REACH[field] if field == FIELDS - 1 else HALO
        for side, peer, has in sides:

            @pl.when(has)
            def _(field=field, reach=reach, side=side, peer=peer):
                halo_copy(field, reach, side, peer).wait_send()
                halo_copy(field, reach, 1 - side, peer).wait_recv()

    lax.fori_loop(0, extent, middle, 0, unroll=2)


def pair_call(tables, index, size, fields, local_rows, width):
    sub = width // TILE
    half = local_rows // COLUMNS
    chunks = fields * CHUNKS
    block = half // CHUNKS * sub
    extent = local_rows + 2 * HALO
    f32 = jnp.float32
    vmem = lambda *shape: pltpu.VMEM(shape, f32)
    pair = lambda *shape: [pltpu.SemaphoreType.DMA(shape)] * 2
    whole = pl.BlockSpec(memory_space=pltpu.VMEM)
    return pl.pallas_call(
        functools.partial(pair_kernel, tables, size, local_rows, sub),
        out_shape=(
            jax.ShapeDtypeStruct((fields * extent * sub, TILE), f32),
            jax.ShapeDtypeStruct((1, REGIONS), f32),
        ),
        in_specs=[whole, pl.BlockSpec(memory_space=pltpu.HBM), whole, pl.BlockSpec(memory_space=pltpu.SMEM)],
        out_specs=(whole, whole),
        scratch_shapes=[
            vmem(fields, local_rows, width),
            vmem(chunks, block, TILE),
            vmem(2, chunks, block, TILE),
            vmem(2, chunks, block, TILE),
            vmem(chunks, block, TILE),
            vmem(chunks, block, TILE),
            vmem(fields * extent * sub, TILE),
            vmem(extent * sub, TILE),
            vmem(REGIONS, local_rows * sub, TILE),
            vmem(REGIONS * 8, TILE),
            vmem(REGIONS * 8, TILE),
            vmem(size, 2 * REGIONS, TILE),
            pltpu.SemaphoreType.DMA((1,)),
        ]
        + pair(chunks)
        + pair(2, chunks)
        + pair(chunks)
        + pair(2, fields)
        + pair(2)
        + pair(2, fields)
        + pair(size),
        compiler_params=pltpu.CompilerParams(
            collective_id=CLASS_ID + index, has_side_effects=True, vmem_limit_bytes=PAIR_VMEM
        ),
    )


def cycle(replica_variables, analysis, labels, pairing):
    size = lax.axis_size("lat")
    members = lax.axis_size("mem")
    fields, local_rows, width = analysis.shape
    sub = width // TILE
    extent = local_rows + 2 * HALO
    extended = jax.ShapeDtypeStruct((fields * extent * sub, TILE), jnp.float32)
    inner = jax.ShapeDtypeStruct((fields * local_rows * sub, TILE), jnp.float32)
    factors = jax.ShapeDtypeStruct((1, REGIONS), jnp.float32)
    patterns = level_patterns(members)
    whole = pl.BlockSpec(memory_space=pltpu.VMEM)
    smem = pl.BlockSpec(memory_space=pltpu.SMEM)
    halo_sems = [pltpu.SemaphoreType.DMA((2, fields)), pltpu.SemaphoreType.DMA((2, fields))]
    buffers = [
        pltpu.VMEM((fields * extent * sub, TILE), jnp.float32),
        pltpu.VMEM((extent * sub, TILE), jnp.float32),
    ]
    state = pl.pallas_call(
        functools.partial(opening_kernel, size, local_rows, sub),
        out_shape=extended,
        in_specs=[pl.BlockSpec(memory_space=pltpu.HBM)],
        out_specs=whole,
        scratch_shapes=[pltpu.VMEM(analysis.shape, jnp.float32), pltpu.SemaphoreType.DMA((fields,))] + halo_sems,
        compiler_params=pltpu.CompilerParams(collective_id=0, has_side_effects=True, vmem_limit_bytes=OPEN_VMEM),
    )(pltpu.with_memory_space_constraint(replica_variables[0], pltpu.HBM))
    first, index = pl.pallas_call(
        functools.partial(first_steps_kernel, size, local_rows, sub, patterns),
        out_shape=(inner, jax.ShapeDtypeStruct((1, 1), jnp.int32)),
        in_specs=[whole, smem],
        out_specs=(whole, smem),
        scratch_shapes=buffers,
        compiler_params=pltpu.CompilerParams(vmem_limit_bytes=PAIR_VMEM),
    )(state, pairing)
    branches = [
        pair_call(slot_tables(edges, members // COLUMNS), k, size, fields, local_rows, width)
        for k, edges in enumerate(patterns)
    ]
    state, factor = lax.switch(
        index[0, 0], branches, first, pltpu.with_memory_space_constraint(analysis, pltpu.HBM), labels, pairing
    )
    closing, factor = pl.pallas_call(
        functools.partial(steps_kernel, size, local_rows, sub, True),
        out_shape=(jax.ShapeDtypeStruct(analysis.shape, jnp.float32), factors),
        in_specs=[whole] * 2,
        out_specs=(whole, whole),
        scratch_shapes=buffers,
        compiler_params=pltpu.CompilerParams(vmem_limit_bytes=VMEM_LIMIT),
    )(state, factor)
    return (closing[None], factor)


def either(replica_variables, analysis, labels, pairing):
    members, rows = lax.axis_size("mem"), analysis.shape[1]
    levels = members // COLUMNS
    fits = members % COLUMNS == 0 and 2 <= levels <= MAX_LEVELS
    if fits and rows == 8 * COLUMNS and rows % (FIELDS * CHUNKS) == 0 and lax.axis_size("lat") > 1:
        return cycle(replica_variables, analysis, labels, pairing)
    return local(replica_variables, analysis, labels, pairing)


def solution(mesh):
    return jax.shard_map(
        either,
        mesh=mesh,
        in_specs=(P("mem", None, "lat", None), P(None, "lat", None), P("lat", None), P()),
        out_specs=(P("mem", None, "lat", None), P("mem", None)),
        check_vma=False,
    )
```

```python
import functools

import jax
import jax.numpy as jnp
from jax import lax
from jax.experimental import pallas as pl
from jax.experimental.pallas import tpu as pltpu
from jax.sharding import PartitionSpec as P

MESH = pl.DeviceIdType.MESH
TILE = 128
REGIONS = 8
STEPS = 3
MAX_BRANCHES = 28
MAX_LEVELS = 4
HALO = 2 * STEPS
VMEM_LIMIT = 24 * 2**20
FIELDS = 4
REACH = (2 * STEPS - 1, 2 * STEPS - 1, 2 * STEPS, STEPS)


grav_coef = 0.1
depth_coef = 0.1
advect_coef = 0.05
diffuse_coef = 0.05
coriolis_coef = 0.05
target_size = 0.5
small_eps = 1e-06


def shift_lon(plane):
    sub = plane.shape[0]
    lane = lax.broadcasted_iota(jnp.int32, plane.shape, 1)
    east = pltpu.roll(plane, TILE - 1, 1)
    east = jnp.where(lane == TILE - 1, pltpu.roll(east, sub - 1, 0), east)
    west = pltpu.roll(plane, 1, 1)
    west = jnp.where(lane == 0, pltpu.roll(west, 1, 0), west)
    return east, west


def diff_lon(plane):
    east, west = shift_lon(plane)
    return east - west


def run_steps(state, buf, spare, local_rows, sub, start, rows_all):
    extent = local_rows + 2 * HALO

    def at(field, e):
        return pl.ds((field * extent + e) * sub, sub)

    def masked(e, plane):
        if HALO <= e < HALO + local_rows:
            return plane
        row = start + (e - HALO)
        return jnp.where((row >= 0) & (row < rows_all), 1.0, 0.0).astype(jnp.float32) * plane

    def coriolis(e):
        row = (start + (e - HALO)).astype(jnp.float32)
        return coriolis_coef * (2.0 * (row + 0.5) / rows_all - 1.0)

    tracer_source, source_field = state, 3
    for step in range(STEPS):
        margin = 2 * (STEPS - 1 - step)
        narrow = STEPS - 1 - step
        target, target_field = (spare, 0) if step % 2 == 0 else (buf, 3)
        own = (HALO, HALO + local_rows)
        for e in range(own[0] - margin - 1, own[1] + margin + 1):
            divergence = diff_lon(state[at(1, e), :]) + state[at(2, e + 1), :] - state[at(2, e - 1), :]
            buf[at(0, e), :] = masked(e, state[at(0, e), :] - depth_coef * divergence)
        for e in range(own[0] - margin, own[1] + margin):
            f = coriolis(e)
            v = state[at(2, e), :]
            u1 = state[at(1, e), :] + f * v - grav_coef * diff_lon(buf[at(0, e), :])
            slope = buf[at(0, e + 1), :] - buf[at(0, e - 1), :]
            buf[at(1, e), :] = u1
            buf[at(2, e), :] = masked(e, v - f * u1 - grav_coef * slope)
        for e in range(own[0] - narrow, own[1] + narrow):
            q = tracer_source[at(source_field, e), :]
            upper = tracer_source[at(source_field, e + 1), :]
            lower = tracer_source[at(source_field, e - 1), :]
            east, west = shift_lon(q)
            advected = buf[at(1, e), :] * (east - west) + buf[at(2, e), :] * (upper - lower)
            spreading = east + west + upper + lower - 4.0 * q
            target[at(target_field, e), :] = masked(e, q - advect_coef * advected + diffuse_coef * spreading)
        state = buf
        tracer_source, source_field = target, target_field
    return [(buf, 0), (buf, 1), (buf, 2), (tracer_source, source_field)]


def pairs_of(size):
    return [(a, b) for a in range(size) for b in range(a + 1, size)]


def pair_index(pairing_ref):
    size = pairing_ref.shape[0]
    me = lax.axis_index("mem")
    partner = pairing_ref[me]
    low, high = jnp.minimum(me, partner), jnp.maximum(me, partner)
    return low * (2 * size - low - 1) // 2 + high - low - 1


def steps_kernel(size, local_rows, sub, as_rows, *refs):
    extent = local_rows + 2 * HALO
    if as_rows:
        state_ref, factor_ref, out_ref, factor_out, buf, spare = refs
        factor_out[...] = factor_ref[...]
    else:
        state_ref, pairing_ref, out_ref, index_ref, buf, spare = refs
        index_ref[0, 0] = pair_index(pairing_ref)
    lat = lax.axis_index("lat")
    fields = run_steps(state_ref, buf, spare, local_rows, sub, lat * local_rows, local_rows * size)
    for field, (ref, place) in enumerate(fields):
        if not as_rows:
            for tile in range(local_rows * sub // 8):
                column = (field * local_rows * sub // 8 + tile) * TILE
                out_ref[:, column : column + TILE] = ref[pl.ds((place * extent + HALO) * sub + tile * 8, 8), :]
            continue
        for row in range(0, local_rows, 8):
            for t in range(sub):
                first = (place * extent + HALO + row) * sub + t
                out_ref[field, row : row + 8, t * TILE : (t + 1) * TILE] = ref[pl.ds(first, 8, stride=sub), :]


def halo_copies(buf, local_rows, sub, lat, size, send_sem, recv_sem):
    extent = local_rows + 2 * HALO
    mem = lax.axis_index("mem")
    copies = []
    for side, peer in ((0, lat - 1), (1, lat + 1)):
        group = []
        for field in range(FIELDS):
            reach = REACH[field]
            source = HALO if side == 0 else HALO + local_rows - reach
            target = HALO + local_rows if side == 0 else HALO - reach
            group.append(
                pltpu.make_async_remote_copy(
                    src_ref=buf.at[pl.ds((field * extent + source) * sub, reach * sub), :],
                    dst_ref=buf.at[pl.ds((field * extent + target) * sub, reach * sub), :],
                    send_sem=send_sem.at[side, field],
                    recv_sem=recv_sem.at[side, field],
                    device_id=(mem, peer),
                    device_id_type=MESH,
                )
            )
        copies.append(group)
    return copies


def clear_outside(buf, local_rows, sub, lat, size):
    extent = local_rows + 2 * HALO
    zeros = jnp.zeros((HALO * sub, TILE), jnp.float32)

    @pl.when(lat == 0)
    def _():
        for field in range(FIELDS):
            buf[pl.ds(field * extent * sub, HALO * sub), :] = zeros

    @pl.when(lat == size - 1)
    def _():
        for field in range(FIELDS):
            buf[pl.ds((field * extent + HALO + local_rows) * sub, HALO * sub), :] = zeros


def start_halo(copies, lat, size):
    for side, has in ((0, lat > 0), (1, lat < size - 1)):

        @pl.when(has)
        def _(side=side):
            for copy in copies[side]:
                copy.start()


def finish_halo(copies, lat, size):
    for side, has in ((0, lat > 0), (1, lat < size - 1)):

        @pl.when(has)
        def _(side=side):
            for copy in copies[side]:
                copy.wait_send()
            for copy in copies[1 - side]:
                copy.wait_recv()


def planes_from_rows(source, buf, local_rows, sub, fields=range(FIELDS)):
    extent = local_rows + 2 * HALO
    for field in fields:
        for row in range(0, local_rows, 8):
            for t in range(sub):
                first = (field * extent + HALO + row) * sub + t
                buf[pl.ds(first, 8, stride=sub), :] = source[field, row : row + 8, t * TILE : (t + 1) * TILE]


def first_kernel(size, local_rows, sub, x_ref, lab_ref, buf, edge_ref, rows, load_sem, send_sem, recv_sem, lab_send, lab_recv):
    lat = lax.axis_index("lat")
    mem = lax.axis_index("mem")
    barrier = pltpu.get_barrier_semaphore()
    for peer, has in ((lat - 1, lat > 0), (lat + 1, lat < size - 1)):

        @pl.when(has)
        def _(peer=peer):
            pl.semaphore_signal(barrier, inc=1, device_id=(mem, peer), device_id_type=MESH)

    loads = [pltpu.make_async_copy(x_ref.at[f], rows.at[f], load_sem.at[f]) for f in range(FIELDS)]
    for load in loads:
        load.start()
    clear_outside(buf, local_rows, sub, lat, size)
    none = jnp.full((sub, TILE), -1.0, jnp.float32)

    @pl.when(lat == 0)
    def _():
        edge_ref[0] = none

    @pl.when(lat == size - 1)
    def _():
        edge_ref[1] = none

    inner = (lat > 0) & (lat < size - 1)

    @pl.when(inner)
    def _():
        pl.semaphore_wait(barrier, 2)

    @pl.when(jnp.logical_not(inner))
    def _():
        pl.semaphore_wait(barrier, 1)

    copies = halo_copies(buf, local_rows, sub, lat, size, send_sem, recv_sem)
    for side, peer in ((0, lat - 1), (1, lat + 1)):
        row = 0 if side == 0 else local_rows - 1
        copies[side].append(
            pltpu.make_async_remote_copy(
                src_ref=lab_ref.at[row],
                dst_ref=edge_ref.at[1 - side],
                send_sem=lab_send.at[side],
                recv_sem=lab_recv.at[side],
                device_id=(mem, peer),
                device_id_type=MESH,
            )
        )
    for field in range(FIELDS + 1):
        if field < FIELDS:
            loads[field].wait()
            planes_from_rows(rows, buf, local_rows, sub, (field,))
        start_halo([side[field : field + 1] for side in copies], lat, size)
    finish_halo(copies, lat, size)


def second_kernel(
    size, local_rows, sub, first_ref, partner_ref, analysis_ref, lab_ref, edge_ref, buf, factor_ref,
    spread, sums, send_sem, recv_sem, sum_send, sum_recv,
):
    lat = lax.axis_index("lat")
    mem = lax.axis_index("mem")
    extent = local_rows + 2 * HALO
    barrier = pltpu.get_barrier_semaphore()
    for hop in range(1, size):
        pl.semaphore_signal(barrier, inc=1, device_id=(mem, lax.rem(lat + hop, size)), device_id_type=MESH)

    def fold(plane):
        total = plane[0:8]
        for i in range(8, sub, 8):
            total = total + plane[i : i + 8]
        return total

    energies = [jnp.zeros((8, TILE), jnp.float32) for _ in range(REGIONS)]
    counts = [jnp.zeros((8, TILE), jnp.float32) for _ in range(REGIONS)]

    def accumulate(row, carry):
        energies, counts = carry
        total = jnp.zeros((sub, TILE), jnp.float32)
        for field in range(FIELDS):
            parts = []
            for i in range(sub // 8):
                column = ((field * local_rows + row) * (sub // 8) + i) * TILE
                place = pl.ds(pl.multiple_of(column, TILE), TILE)
                parts.append(first_ref[:, place] - partner_ref[:, place])
            half = 0.5 * jnp.concatenate(parts, axis=0)
            spread[field, row] = half
            total = total + half * half
        quarter = 0.125 * total
        here = lab_ref[row]
        before = jnp.where(row == 0, edge_ref[0], lab_ref[jnp.maximum(row - 1, 0)])
        after = jnp.where(row == local_rows - 1, edge_ref[1], lab_ref[jnp.minimum(row + 1, local_rows - 1)])
        new_energies, new_counts = [], []
        for k in range(REGIONS):
            kept = jnp.where(here == k, 1.0, 0.0)
            weight = 2.0 * kept + jnp.where(before == k, 1.0, 0.0) + jnp.where(after == k, 1.0, 0.0)
            new_energies.append(energies[k] + fold(quarter * weight))
            new_counts.append(counts[k] + fold(kept))
        return new_energies, new_counts

    energies, counts = lax.fori_loop(0, local_rows, accumulate, (energies, counts))
    for k in range(REGIONS):
        sums[0, k : k + 1, :] = jnp.sum(energies[k], axis=0, keepdims=True)
        sums[0, REGIONS + k : REGIONS + k + 1, :] = jnp.sum(counts[k], axis=0, keepdims=True)

    pl.semaphore_wait(barrier, size - 1)
    sends = []
    for hop in range(1, size):
        sends.append(
            pltpu.make_async_remote_copy(
                src_ref=sums.at[0],
                dst_ref=sums.at[hop],
                send_sem=sum_send.at[hop],
                recv_sem=sum_recv.at[hop],
                device_id=(mem, lax.rem(lat + hop, size)),
                device_id_type=MESH,
            )
        )
    for copy in sends:
        copy.start()
    clear_outside(buf, local_rows, sub, lat, size)
    planes_from_rows(analysis_ref, buf, local_rows, sub)
    for copy in sends:
        copy.wait()
    total = sums[0]
    for hop in range(1, size):
        total = total + sums[hop]
    total = jnp.sum(total, axis=1, keepdims=True)
    factor = target_size / jnp.sqrt(total[:REGIONS] / total[REGIONS:] + small_eps)
    wide = jnp.broadcast_to(factor, (REGIONS, TILE))
    diagonal = lax.broadcasted_iota(jnp.int32, (REGIONS, TILE), 0) == lax.broadcasted_iota(
        jnp.int32, (REGIONS, TILE), 1
    )
    factor_ref[...] = jnp.sum(jnp.where(diagonal, wide, 0.0), axis=0, keepdims=True)[:, :REGIONS]
    lanes = [jnp.broadcast_to(wide[k : k + 1], (sub, TILE)) for k in range(REGIONS)]

    def middle(row, carry):
        here = lab_ref[row]
        scale = lanes[0]
        for k in range(1, REGIONS):
            scale = jnp.where(here == k, lanes[k], scale)
        for field in range(FIELDS):
            place = pl.ds(pl.multiple_of((field * extent + HALO + row) * sub, sub), sub)
            buf[place, :] = buf[place, :] + scale * spread[field, row]
        return carry

    lax.fori_loop(0, local_rows, middle, 0)
    copies = halo_copies(buf, local_rows, sub, lat, size, send_sem, recv_sem)
    start_halo(copies, lat, size)
    finish_halo(copies, lat, size)


def partner_fields(fields, pairing, index):
    pairs = pairs_of(lax.axis_size("mem"))
    if len(pairs) > MAX_BRANCHES:
        piece = lax.all_gather(fields, "mem", axis=0)
        return lax.dynamic_index_in_dim(piece, pairing[lax.axis_index("mem")], 0, keepdims=False)
    branches = [
        functools.partial(lax.ppermute, axis_name="mem", perm=[(a, b), (b, a)]) for a, b in pairs
    ]
    return lax.switch(index, branches, fields)


def local(replica_variables, analysis, labels, pairing):
    size = lax.axis_size("lat")
    fields, local_rows, width = analysis.shape
    sub = width // TILE
    extent = local_rows + 2 * HALO
    wide = jax.ShapeDtypeStruct((8, fields * local_rows * width // 8), jnp.float32)
    extended = jax.ShapeDtypeStruct((fields * extent * sub, TILE), jnp.float32)
    edges = jax.ShapeDtypeStruct((2, sub, TILE), jnp.float32)
    factors = jax.ShapeDtypeStruct((1, REGIONS), jnp.float32)
    label_planes = jnp.broadcast_to(labels.astype(jnp.float32)[..., None], (local_rows, sub, TILE))
    whole = pl.BlockSpec(memory_space=pltpu.VMEM)
    buffers = [
        pltpu.VMEM((fields * extent * sub, TILE), jnp.float32),
        pltpu.VMEM((extent * sub, TILE), jnp.float32),
    ]
    halo_sems = [pltpu.SemaphoreType.DMA((2, fields)), pltpu.SemaphoreType.DMA((2, fields))]
    state, edge = pl.pallas_call(
        functools.partial(first_kernel, size, local_rows, sub),
        out_shape=(extended, edges),
        in_specs=[pl.BlockSpec(memory_space=pltpu.HBM), whole],
        out_specs=(whole, whole),
        scratch_shapes=[pltpu.VMEM(analysis.shape, jnp.float32), pltpu.SemaphoreType.DMA((fields,))]
        + halo_sems
        + [pltpu.SemaphoreType.DMA((2,)), pltpu.SemaphoreType.DMA((2,))],
        compiler_params=pltpu.CompilerParams(collective_id=0, has_side_effects=True, vmem_limit_bytes=VMEM_LIMIT),
    )(replica_variables[0], label_planes)
    smem = pl.BlockSpec(memory_space=pltpu.SMEM)
    first, index = pl.pallas_call(
        functools.partial(steps_kernel, size, local_rows, sub, False),
        out_shape=(wide, jax.ShapeDtypeStruct((1, 1), jnp.int32)),
        in_specs=[whole, smem],
        out_specs=(whole, smem),
        scratch_shapes=buffers,
        compiler_params=pltpu.CompilerParams(vmem_limit_bytes=VMEM_LIMIT),
    )(state, pairing)
    partner = partner_fields(first, pairing, index[0, 0])
    state, factor = pl.pallas_call(
        functools.partial(second_kernel, size, local_rows, sub),
        out_shape=(extended, factors),
        in_specs=[whole] * 5,
        out_specs=(whole, whole),
        scratch_shapes=[
            pltpu.VMEM((fields, local_rows, sub, TILE), jnp.float32),
            pltpu.VMEM((size, 2 * REGIONS, TILE), jnp.float32),
        ]
        + halo_sems
        + [pltpu.SemaphoreType.DMA((size,)), pltpu.SemaphoreType.DMA((size,))],
        compiler_params=pltpu.CompilerParams(collective_id=1, has_side_effects=True, vmem_limit_bytes=VMEM_LIMIT),
    )(first, partner, analysis, label_planes, edge)
    closing, factor = pl.pallas_call(
        functools.partial(steps_kernel, size, local_rows, sub, True),
        out_shape=(jax.ShapeDtypeStruct(analysis.shape, jnp.float32), factors),
        in_specs=[whole] * 2,
        out_specs=(whole, whole),
        scratch_shapes=buffers,
        compiler_params=pltpu.CompilerParams(vmem_limit_bytes=VMEM_LIMIT),
    )(state, factor)
    return (closing[None], factor)


CLASS_ID = 2
ORDER = (2, 1, 0, 3)
COLUMNS = 2
CHUNKS = 2
PAIR_VMEM = 16 * 2**20


def matchings(items):
    if not items:
        return [()]
    head, found = items[0], []
    for i in range(1, len(items)):
        for rest in matchings(items[1:i] + items[i + 1 :]):
            found.append(((head, items[i]),) + rest)
    return found


def level_edges(matching):
    return tuple(sorted(tuple(sorted((a // COLUMNS, b // COLUMNS))) for a, b in matching))


def level_patterns(size):
    return sorted({level_edges(m) for m in matchings(tuple(range(size)))})


def slot_tables(edges, levels):
    peer = [[z, z] for z in range(levels)]
    slot = [[0, 1] for _ in range(levels)]
    moves = [0] * levels
    used = [0] * levels
    for a, b in edges:
        if a == b:
            continue
        i, j = used[a], used[b]
        used[a] += 1
        used[b] += 1
        peer[a][i], slot[a][i] = b, j
        peer[b][j], slot[b][j] = a, i
        moves[a] = moves[b] = 1
    return peer, slot, moves


def pattern_index(patterns, pairing_ref):
    members = pairing_ref.shape[0]
    levels = members // COLUMNS
    level = [lax.div(pairing_ref[m], COLUMNS) for m in range(members)]
    count = {}
    for a in range(levels):
        for b in range(a + 1, levels):
            count[a, b] = sum(jnp.where(level[a * COLUMNS + i] == b, 1, 0) for i in range(COLUMNS))
    index = jnp.int32(0)
    for k, edges in enumerate(patterns):
        good = None
        for pair, n in count.items():
            same = n == sum(e == pair for e in edges)
            good = same if good is None else good & same
        index = jnp.where(good, k, index)
    return index


def lookup(index, table):
    value = jnp.int32(table[0])
    for k, entry in enumerate(table):
        if k and entry != table[0]:
            value = jnp.where(index == k, entry, value)
    return value


class Flow:
    def __init__(self, local_rows, sub, start, rows_all):
        self.local_rows, self.sub, self.start, self.rows_all = local_rows, sub, start, rows_all
        self.extent = local_rows + 2 * HALO

    def at(self, field, e):
        return pl.ds((field * self.extent + e) * self.sub, self.sub)

    def owns(self, e):
        return HALO <= e < HALO + self.local_rows

    def masked(self, e, values):
        if self.owns(e):
            return values
        row = self.start + (e - HALO)
        return jnp.where((row >= 0) & (row < self.rows_all), 1.0, 0.0).astype(jnp.float32) * values

    def height(self, source, e):
        divergence = diff_lon(source[self.at(1, e), :]) + source[self.at(2, e + 1), :] - source[self.at(2, e - 1), :]
        return self.masked(e, source[self.at(0, e), :] - depth_coef * divergence)

    def wind(self, source, heights, e):
        row = (self.start + (e - HALO)).astype(jnp.float32)
        f = coriolis_coef * (2.0 * (row + 0.5) / self.rows_all - 1.0)
        v = source[self.at(2, e), :]
        u1 = source[self.at(1, e), :] + f * v - grav_coef * diff_lon(heights[self.at(0, e), :])
        slope = heights[self.at(0, e + 1), :] - heights[self.at(0, e - 1), :]
        return u1, self.masked(e, v - f * u1 - grav_coef * slope)

    def tracer(self, source, place, u1, v1, e):
        q = source[self.at(place, e), :]
        upper, lower = source[self.at(place, e + 1), :], source[self.at(place, e - 1), :]
        east, west = shift_lon(q)
        advected = u1 * (east - west) + v1 * (upper - lower)
        spreading = east + west + upper + lower - 4.0 * q
        return self.masked(e, q - advect_coef * advected + diffuse_coef * spreading)


def flow_steps(flow, state, buf, spare, keep, flow_halo, tracer_halo, flow_done):
    low, high = HALO, HALO + flow.local_rows
    source, place, tracer_source = state, 3, state
    for step in range(STEPS):
        margin = 2 * (STEPS - 1 - step)
        narrow = STEPS - 1 - step
        last = step == STEPS - 1
        target, spot = (spare, 0) if step % 2 == 0 else (buf, 3)

        def heights(rows, source=source, last=last):
            for e in rows:
                value = flow.height(source, e)
                buf[flow.at(0, e), :] = value
                if last and keep is not None and flow.owns(e):
                    keep(0, e, value)

        def winds(rows, source=source, last=last):
            for e in rows:
                u1, v1 = flow.wind(source, buf, e)
                buf[flow.at(1, e), :] = u1
                buf[flow.at(2, e), :] = v1
                if last and keep is not None:
                    keep(1, e, u1)
                    keep(2, e, v1)

        def tracers(rows, last=last, tracer_source=tracer_source, place=place, target=target, spot=spot):
            for e in rows:
                value = flow.tracer(tracer_source, place, buf[flow.at(1, e), :], buf[flow.at(2, e), :], e)
                if last and keep is not None:
                    keep(3, e, value)
                else:
                    target[flow.at(spot, e), :] = value

        def run(piece, lower, upper, inner):
            if inner is None:
                piece(range(lower, upper))
            else:
                piece(range(lower, inner[0]))
                piece(range(inner[1], upper))

        early = step == 0 and flow_halo is not None
        inner = [None] * 3
        if early:
            inner = [(low + 1, high - 1), (low + 2, high - 2), (low + 2, high - 2)]
            for piece, rows in zip((heights, winds, tracers), inner):
                piece(range(*rows))
            flow_halo()
        run(heights, low - margin - 1, high + margin + 1, inner[0])
        run(winds, low - margin, high + margin, inner[1])
        if early:
            tracer_halo()
        if last and flow_done is not None:
            flow_done()
        run(tracers, low - narrow, high + narrow, inner[2])
        source, tracer_source, place = buf, target, spot
    return tracer_source, place


def opening_kernel(
    size, local_rows, sub, patterns, x_ref, pairing_ref, out_ref, index_ref,
    state, buf, spare, rows, load_sem, send_sem, recv_sem,
):
    lat = lax.axis_index("lat")
    mem = lax.axis_index("mem")
    barrier = pltpu.get_barrier_semaphore()
    for peer, has in ((lat - 1, lat > 0), (lat + 1, lat < size - 1)):

        @pl.when(has)
        def _(peer=peer):
            pl.semaphore_signal(barrier, inc=1, device_id=(mem, peer), device_id_type=MESH)

    loads = [pltpu.make_async_copy(x_ref.at[f], rows.at[f], load_sem.at[f]) for f in range(FIELDS)]
    for f in ORDER:
        loads[f].start()
    index_ref[0, 0] = pattern_index(patterns, pairing_ref)
    clear_outside(state, local_rows, sub, lat, size)
    inner = (lat > 0) & (lat < size - 1)

    @pl.when(inner)
    def _():
        pl.semaphore_wait(barrier, 2)

    @pl.when(jnp.logical_not(inner))
    def _():
        pl.semaphore_wait(barrier, 1)

    copies = halo_copies(state, local_rows, sub, lat, size, send_sem, recv_sem)
    for f in ORDER:
        loads[f].wait()
        planes_from_rows(rows, state, local_rows, sub, (f,))
        start_halo([side[f : f + 1] for side in copies], lat, size)

    def received(fields):
        for side, has in ((0, lat > 0), (1, lat < size - 1)):

            @pl.when(has)
            def _(side=side):
                for f in fields:
                    copies[1 - side][f].wait_recv()

    def keep(field, e, value):
        out_ref[pl.ds((field * local_rows + e - HALO) * sub, sub), :] = value

    flow = Flow(local_rows, sub, lat * local_rows, local_rows * size)
    flow_steps(flow, state, buf, spare, keep, lambda: received(ORDER[:3]), lambda: received(ORDER[3:]), None)
    for side, has in ((0, lat > 0), (1, lat < size - 1)):

        @pl.when(has)
        def _(side=side):
            for copy in copies[side]:
                copy.wait_send()


def plane(sub, index):
    return pl.ds(pl.multiple_of(index * sub, sub), sub)


def fold(block):
    total = block[0:8]
    for i in range(8, block.shape[0], 8):
        total = total + block[i : i + 8]
    return total


def pair_kernel(
    tables, size, local_rows, sub,
    first_ref, analysis_ref, lab_ref, pairing_ref,
    state, factor_ref,
    av, near, send, came, onward, final, spread, labels, weights, energy, tally, sums,
    load_sem, near_send, near_recv, z_send, z_recv, last_send, last_recv,
    ana_send, ana_recv, lab_send, lab_recv, halo_send, halo_recv, sum_send, sum_recv,
):
    lat = lax.axis_index("lat")
    mem = lax.axis_index("mem")
    z, y = lax.div(mem, COLUMNS), lax.rem(mem, COLUMNS)
    peer_table, slot_table, moves_table = tables
    levels = len(moves_table)
    half = local_rows // COLUMNS
    deep = half // CHUNKS
    block = deep * sub
    chunks = FIELDS * CHUNKS
    extent = local_rows + 2 * HALO
    other = (z * COLUMNS + 1 - y, lat)
    peers = [lookup(z, [peer_table[k][j] for k in range(levels)]) for j in range(2)]
    slots = [lookup(z, [slot_table[k][j] for k in range(levels)]) for j in range(2)]
    moves = lookup(z, moves_table) == 1

    load = pltpu.make_async_copy(analysis_ref, av, load_sem.at[0])
    load.start()
    barrier = pltpu.get_barrier_semaphore()
    pl.semaphore_signal(barrier, inc=1, device_id=other, device_id_type=MESH)

    @pl.when(moves)
    def _():
        for j in range(2):
            pl.semaphore_signal(barrier, inc=1, device_id=(peers[j] * COLUMNS + y, lat), device_id_type=MESH)

    for hop in range(1, size):
        pl.semaphore_signal(barrier, inc=1, device_id=(mem, lax.rem(lat + hop, size)), device_id_type=MESH)
    clear_outside(state, local_rows, sub, lat, size)
    clear_outside(spread, local_rows, sub, lat, size)
    none = jnp.full((HALO * sub, TILE), -1.0, jnp.float32)

    @pl.when(lat == 0)
    def _():
        labels[pl.ds(0, HALO * sub), :] = none

    @pl.when(lat == size - 1)
    def _():
        labels[pl.ds((HALO + local_rows) * sub, HALO * sub), :] = none

    @pl.when(moves)
    def _():
        pl.semaphore_wait(barrier, size + 2)

    @pl.when(jnp.logical_not(moves))
    def _():
        pl.semaphore_wait(barrier, size)

    def rows_of(c, column):
        field, part = lax.div(c, CHUNKS), lax.rem(c, CHUNKS)
        return pl.ds(pl.multiple_of((field * local_rows + column * half + part * deep) * sub, sub), block)

    def near_copy(c):
        return pltpu.make_async_remote_copy(
            src_ref=first_ref.at[rows_of(c, 1 - y), :],
            dst_ref=near.at[c],
            send_sem=near_send.at[c],
            recv_sem=near_recv.at[c],
            device_id=other,
            device_id_type=MESH,
        )

    def cross_copy(c, j, slot):
        return pltpu.make_async_remote_copy(
            src_ref=send.at[j, c],
            dst_ref=came.at[slot, c],
            send_sem=z_send.at[j, c],
            recv_sem=z_recv.at[slot, c],
            device_id=(peers[j] * COLUMNS + y, lat),
            device_id_type=MESH,
        )

    def last_copy(c):
        return pltpu.make_async_remote_copy(
            src_ref=onward.at[c],
            dst_ref=final.at[c],
            send_sem=last_send.at[c],
            recv_sem=last_recv.at[c],
            device_id=other,
            device_id_type=MESH,
        )

    def halo_copy(field, reach, side, peer):
        source = HALO if side == 0 else HALO + local_rows - reach
        target = HALO + local_rows if side == 0 else HALO - reach
        return pltpu.make_async_remote_copy(
            src_ref=spread.at[pl.ds(pl.multiple_of((field * extent + source) * sub, sub), reach * sub), :],
            dst_ref=spread.at[pl.ds(pl.multiple_of((field * extent + target) * sub, sub), reach * sub), :],
            send_sem=halo_send.at[side, field],
            recv_sem=halo_recv.at[side, field],
            device_id=(mem, peer),
            device_id_type=MESH,
        )

    def start_near(c, carry):
        near_copy(c).start()
        return carry

    lax.fori_loop(0, chunks, start_near, 0)

    pick = [pairing_ref[z * COLUMNS + i] for i in range(COLUMNS)]
    pick_level = [lax.div(p, COLUMNS) for p in pick]
    first_slot_item = jnp.where(pick_level[0] == peers[0], 0, 1)
    here_level = jnp.where(y == 0, pick_level[0], pick_level[1])
    here_column = lax.rem(jnp.where(y == 0, pick[0], pick[1]), COLUMNS)
    keep_slot = jnp.where(peers[0] == peers[1], here_column, jnp.where(here_level == peers[0], 0, 1))
    own_first = jnp.full((sub, TILE), first_slot_item, jnp.int32) == y
    keep_first = jnp.full((sub, TILE), keep_slot, jnp.int32) == 0
    diagonal = lax.broadcasted_iota(jnp.int32, (sub, sub), 0) == lax.broadcasted_iota(jnp.int32, (sub, sub), 1)

    def label_row(row, carry):
        line = jnp.broadcast_to(lab_ref[pl.ds(row, 1), :].astype(jnp.float32), (sub, sub))
        column = jnp.sum(jnp.where(diagonal, line, 0.0), axis=1, keepdims=True)
        labels[plane(sub, HALO + row), :] = jnp.broadcast_to(column, (sub, TILE))
        return carry

    lax.fori_loop(0, local_rows, label_row, 0, unroll=4)
    lab_copies = [
        [
            pltpu.make_async_remote_copy(
                src_ref=labels.at[pl.ds(HALO * sub if side == 0 else local_rows * sub, HALO * sub), :],
                dst_ref=labels.at[pl.ds((HALO + local_rows) * sub if side == 0 else 0, HALO * sub), :],
                send_sem=lab_send.at[side],
                recv_sem=lab_recv.at[side],
                device_id=(mem, peer),
                device_id_type=MESH,
            )
        ]
        for side, peer in ((0, lat - 1), (1, lat + 1))
    ]
    start_halo(lab_copies, lat, size)
    load.wait()
    tiles = FIELDS * sub // chunks

    def lay_out(c):
        for i in range(tiles):
            index = c * tiles + i
            field, tile = lax.div(index, sub), lax.rem(index, sub)
            for row in range(0, local_rows, 8):
                state[pl.ds((field * extent + HALO + row) * sub + tile, 8, stride=sub), :] = av[
                    field, row : row + 8, pl.ds(pl.multiple_of(tile * TILE, TILE), TILE)
                ]

    def cross(c, carry):
        near_copy(c).wait_recv()

        @pl.when(moves)
        def _():
            start = rows_of(c, y).start
            for r in range(deep):
                here = pl.ds(r * sub, sub)
                a = first_ref[pl.ds(pl.multiple_of(start + r * sub, sub), sub), :]
                b = near[c, here, :]
                send[0, c, here, :] = jnp.where(own_first, a, b)
                send[1, c, here, :] = jnp.where(own_first, b, a)
            for j in range(2):
                cross_copy(c, j, slots[j]).start()

        lay_out(c)
        return carry

    lax.fori_loop(0, chunks, cross, 0)
    ana_copies = halo_copies(state, local_rows, sub, lat, size, ana_send, ana_recv)
    start_halo(ana_copies, lat, size)
    finish_halo(lab_copies, lat, size)

    def weigh(row, counts):
        here = labels[plane(sub, HALO + row), :]
        before = labels[plane(sub, HALO + row - 1), :]
        after = labels[plane(sub, HALO + row + 1), :]
        new = []
        for k in range(REGIONS):
            kept = jnp.where(here == k, 1.0, 0.0)
            around = jnp.where(before == k, 0.125, 0.0) + jnp.where(after == k, 0.125, 0.0)
            weights[k, plane(sub, row), :] = 0.25 * kept + around
            new.append(counts[k] + fold(kept))
        return new

    counts = lax.fori_loop(0, local_rows, weigh, [jnp.zeros((8, TILE), jnp.float32) for _ in range(REGIONS)])
    for k in range(REGIONS):
        tally[pl.ds(k * 8, 8), :] = counts[k]
    energy[...] = jnp.zeros_like(energy)

    def absorb(field, first_row, theirs):
        totals = [energy[pl.ds(k * 8, 8), :] for k in range(REGIONS)]
        for r in range(deep):
            row = first_row + r
            value = 0.5 * (first_ref[plane(sub, field * local_rows + row), :] - theirs[r * sub : (r + 1) * sub, :])
            spread[plane(sub, field * extent + HALO + row), :] = value
            square = value * value
            for k in range(REGIONS):
                totals[k] = totals[k] + fold(square * weights[k, plane(sub, row), :])
        for k in range(REGIONS):
            energy[pl.ds(k * 8, 8), :] = totals[k]

    def forward(field, part):
        c = field * CHUNKS + part

        @pl.when(moves)
        def _():
            for j in range(2):
                cross_copy(c, j, j).wait_recv()
            for r in range(deep):
                here = pl.ds(r * sub, sub)
                a = came[0, c, here, :]
                b = came[1, c, here, :]
                onward[c, here, :] = jnp.where(keep_first, b, a)
                near[c, here, :] = jnp.where(keep_first, a, b)

        @pl.when(jnp.logical_not(moves))
        def _():
            onward[c] = first_ref[rows_of(c, y), :]

        last_copy(c).start()

        absorb(field, y * half + part * deep, near.at[c])

    def arrive(field, part):
        c = field * CHUNKS + part
        last_copy(c).wait_recv()
        absorb(field, (1 - y) * half + part * deep, final.at[c])

    sides = ((0, lat - 1, lat > 0), (1, lat + 1, lat < size - 1))

    def send_halo(field, reach):
        for side, peer, has in sides:

            @pl.when(has)
            def _(side=side, peer=peer):
                halo_copy(field, reach, side, peer).start()

    def stage(c, carry):
        @pl.when(c < chunks)
        def _():
            forward(lax.div(c, CHUNKS), lax.rem(c, CHUNKS))

        @pl.when(c > 0)
        def _():
            field, part = lax.div(c - 1, CHUNKS), lax.rem(c - 1, CHUNKS)
            arrive(field, part)

            @pl.when((part == CHUNKS - 1) & (field < FIELDS - 1))
            def _():
                send_halo(field, HALO)

        return carry

    lax.fori_loop(0, chunks + 1, stage, 0)
    for k in range(REGIONS):
        for i, table in enumerate((energy, tally)):
            sums[0, i * REGIONS + k : i * REGIONS + k + 1, :] = jnp.sum(
                table[pl.ds(k * 8, 8), :], axis=0, keepdims=True
            )
    shares = [
        pltpu.make_async_remote_copy(
            src_ref=sums.at[0],
            dst_ref=sums.at[hop],
            send_sem=sum_send.at[hop],
            recv_sem=sum_recv.at[hop],
            device_id=(mem, lax.rem(lat + hop, size)),
            device_id_type=MESH,
        )
        for hop in range(1, size)
    ]
    for copy in shares:
        copy.start()
    send_halo(FIELDS - 1, REACH[FIELDS - 1])
    finish_halo(ana_copies, lat, size)

    def finish(c, carry):
        near_copy(c).wait_send()
        last_copy(c).wait_send()

        @pl.when(moves)
        def _():
            for j in range(2):
                cross_copy(c, j, j).wait_send()

        return carry

    lax.fori_loop(0, chunks, finish, 0)
    for copy in shares:
        copy.wait()
    total = sums[0]
    for hop in range(1, size):
        total = total + sums[hop]
    total = jnp.sum(total, axis=1, keepdims=True)
    factor = target_size / jnp.sqrt(total[:REGIONS] / total[REGIONS:] + small_eps)
    wide = jnp.broadcast_to(factor, (REGIONS, TILE))
    corner = lax.broadcasted_iota(jnp.int32, (REGIONS, TILE), 0) == lax.broadcasted_iota(
        jnp.int32, (REGIONS, TILE), 1
    )
    factor_ref[...] = jnp.sum(jnp.where(corner, wide, 0.0), axis=0, keepdims=True)[:, :REGIONS]
    lanes = [jnp.broadcast_to(wide[k : k + 1], (sub, TILE)) for k in range(REGIONS)]

    def middle(e, carry):
        here = labels[plane(sub, e), :]
        scale = lanes[0]
        for k in range(1, REGIONS):
            scale = jnp.where(here == k, lanes[k], scale)
        for field in range(FIELDS):
            place = plane(sub, field * extent + e)
            state[place, :] = state[place, :] + scale * spread[place, :]
        return carry

    lax.fori_loop(HALO, HALO + local_rows, middle, 0, unroll=2)
    for field in range(FIELDS):
        reach = REACH[field] if field == FIELDS - 1 else HALO
        for side, peer, has in sides:

            @pl.when(has)
            def _(field=field, reach=reach, side=side, peer=peer):
                halo_copy(field, reach, side, peer).wait_send()
                halo_copy(field, reach, 1 - side, peer).wait_recv()

    lax.fori_loop(0, HALO, middle, 0, unroll=2)
    lax.fori_loop(HALO + local_rows, extent, middle, 0, unroll=2)


def pair_call(tables, index, size, fields, local_rows, width):
    sub = width // TILE
    half = local_rows // COLUMNS
    chunks = fields * CHUNKS
    block = half // CHUNKS * sub
    extent = local_rows + 2 * HALO
    f32 = jnp.float32
    vmem = lambda *shape: pltpu.VMEM(shape, f32)
    pair = lambda *shape: [pltpu.SemaphoreType.DMA(shape)] * 2
    whole = pl.BlockSpec(memory_space=pltpu.VMEM)
    return pl.pallas_call(
        functools.partial(pair_kernel, tables, size, local_rows, sub),
        out_shape=(
            jax.ShapeDtypeStruct((fields * extent * sub, TILE), f32),
            jax.ShapeDtypeStruct((1, REGIONS), f32),
        ),
        in_specs=[whole, pl.BlockSpec(memory_space=pltpu.HBM), whole, pl.BlockSpec(memory_space=pltpu.SMEM)],
        out_specs=(whole, whole),
        scratch_shapes=[
            vmem(fields, local_rows, width),
            vmem(chunks, block, TILE),
            vmem(2, chunks, block, TILE),
            vmem(2, chunks, block, TILE),
            vmem(chunks, block, TILE),
            vmem(chunks, block, TILE),
            vmem(fields * extent * sub, TILE),
            vmem(extent * sub, TILE),
            vmem(REGIONS, local_rows * sub, TILE),
            vmem(REGIONS * 8, TILE),
            vmem(REGIONS * 8, TILE),
            vmem(size, 2 * REGIONS, TILE),
            pltpu.SemaphoreType.DMA((1,)),
        ]
        + pair(chunks)
        + pair(2, chunks)
        + pair(chunks)
        + pair(2, fields)
        + pair(2)
        + pair(2, fields)
        + pair(size),
        compiler_params=pltpu.CompilerParams(
            collective_id=CLASS_ID + index, has_side_effects=True, vmem_limit_bytes=PAIR_VMEM
        ),
    )


def cycle(replica_variables, analysis, labels, pairing):
    size = lax.axis_size("lat")
    members = lax.axis_size("mem")
    fields, local_rows, width = analysis.shape
    sub = width // TILE
    extent = local_rows + 2 * HALO
    inner = jax.ShapeDtypeStruct((fields * local_rows * sub, TILE), jnp.float32)
    factors = jax.ShapeDtypeStruct((1, REGIONS), jnp.float32)
    patterns = level_patterns(members)
    whole = pl.BlockSpec(memory_space=pltpu.VMEM)
    smem = pl.BlockSpec(memory_space=pltpu.SMEM)
    halo_sems = [pltpu.SemaphoreType.DMA((2, fields)), pltpu.SemaphoreType.DMA((2, fields))]
    buffers = [
        pltpu.VMEM((fields * extent * sub, TILE), jnp.float32),
        pltpu.VMEM((extent * sub, TILE), jnp.float32),
    ]
    first, index = pl.pallas_call(
        functools.partial(opening_kernel, size, local_rows, sub, patterns),
        out_shape=(inner, jax.ShapeDtypeStruct((1, 1), jnp.int32)),
        in_specs=[pl.BlockSpec(memory_space=pltpu.HBM), smem],
        out_specs=(whole, smem),
        scratch_shapes=[pltpu.VMEM((fields * extent * sub, TILE), jnp.float32)]
        + buffers
        + [pltpu.VMEM(analysis.shape, jnp.float32), pltpu.SemaphoreType.DMA((fields,))]
        + halo_sems,
        compiler_params=pltpu.CompilerParams(collective_id=0, has_side_effects=True, vmem_limit_bytes=PAIR_VMEM),
    )(pltpu.with_memory_space_constraint(replica_variables[0], pltpu.HBM), pairing)
    branches = [
        pair_call(slot_tables(edges, members // COLUMNS), k, size, fields, local_rows, width)
        for k, edges in enumerate(patterns)
    ]
    state, factor = lax.switch(
        index[0, 0], branches, first, pltpu.with_memory_space_constraint(analysis, pltpu.HBM), labels, pairing
    )
    closing, factor = pl.pallas_call(
        functools.partial(steps_kernel, size, local_rows, sub, True),
        out_shape=(jax.ShapeDtypeStruct(analysis.shape, jnp.float32), factors),
        in_specs=[whole] * 2,
        out_specs=(whole, whole),
        scratch_shapes=buffers,
        compiler_params=pltpu.CompilerParams(vmem_limit_bytes=VMEM_LIMIT),
    )(state, factor)
    return (closing[None], factor)


def either(replica_variables, analysis, labels, pairing):
    members, rows = lax.axis_size("mem"), analysis.shape[1]
    levels = members // COLUMNS
    fits = members % COLUMNS == 0 and 2 <= levels <= MAX_LEVELS
    if fits and rows == 8 * COLUMNS and rows % (FIELDS * CHUNKS) == 0 and lax.axis_size("lat") > 1:
        return cycle(replica_variables, analysis, labels, pairing)
    return local(replica_variables, analysis, labels, pairing)


def solution(mesh):
    return jax.shard_map(
        either,
        mesh=mesh,
        in_specs=(P("mem", None, "lat", None), P(None, "lat", None), P("lat", None), P()),
        out_specs=(P("mem", None, "lat", None), P("mem", None)),
        check_vma=False,
    )
```

```python
import functools

import jax
import jax.numpy as jnp
from jax import lax
from jax.experimental import pallas as pl
from jax.experimental.pallas import tpu as pltpu
from jax.sharding import PartitionSpec as P

MESH = pl.DeviceIdType.MESH
TILE = 128
REGIONS = 8
STEPS = 3
MAX_BRANCHES = 28
MAX_LEVELS = 4
HALO = 2 * STEPS
VMEM_LIMIT = 24 * 2**20
FIELDS = 4
REACH = (2 * STEPS - 1, 2 * STEPS - 1, 2 * STEPS, STEPS)


grav_coef = 0.1
depth_coef = 0.1
advect_coef = 0.05
diffuse_coef = 0.05
coriolis_coef = 0.05
target_size = 0.5
small_eps = 1e-06


def shift_lon(plane):
    sub = plane.shape[0]
    lane = lax.broadcasted_iota(jnp.int32, plane.shape, 1)
    east = pltpu.roll(plane, TILE - 1, 1)
    east = jnp.where(lane == TILE - 1, pltpu.roll(east, sub - 1, 0), east)
    west = pltpu.roll(plane, 1, 1)
    west = jnp.where(lane == 0, pltpu.roll(west, 1, 0), west)
    return east, west


def diff_lon(plane):
    east, west = shift_lon(plane)
    return east - west


def run_steps(state, buf, spare, local_rows, sub, start, rows_all):
    extent = local_rows + 2 * HALO

    def at(field, e):
        return pl.ds((field * extent + e) * sub, sub)

    def masked(e, plane):
        if HALO <= e < HALO + local_rows:
            return plane
        row = start + (e - HALO)
        return jnp.where((row >= 0) & (row < rows_all), 1.0, 0.0).astype(jnp.float32) * plane

    def coriolis(e):
        row = (start + (e - HALO)).astype(jnp.float32)
        return coriolis_coef * (2.0 * (row + 0.5) / rows_all - 1.0)

    tracer_source, source_field = state, 3
    for step in range(STEPS):
        margin = 2 * (STEPS - 1 - step)
        narrow = STEPS - 1 - step
        target, target_field = (spare, 0) if step % 2 == 0 else (buf, 3)
        own = (HALO, HALO + local_rows)
        for e in range(own[0] - margin - 1, own[1] + margin + 1):
            divergence = diff_lon(state[at(1, e), :]) + state[at(2, e + 1), :] - state[at(2, e - 1), :]
            buf[at(0, e), :] = masked(e, state[at(0, e), :] - depth_coef * divergence)
        for e in range(own[0] - margin, own[1] + margin):
            f = coriolis(e)
            v = state[at(2, e), :]
            u1 = state[at(1, e), :] + f * v - grav_coef * diff_lon(buf[at(0, e), :])
            slope = buf[at(0, e + 1), :] - buf[at(0, e - 1), :]
            buf[at(1, e), :] = u1
            buf[at(2, e), :] = masked(e, v - f * u1 - grav_coef * slope)
        for e in range(own[0] - narrow, own[1] + narrow):
            q = tracer_source[at(source_field, e), :]
            upper = tracer_source[at(source_field, e + 1), :]
            lower = tracer_source[at(source_field, e - 1), :]
            east, west = shift_lon(q)
            advected = buf[at(1, e), :] * (east - west) + buf[at(2, e), :] * (upper - lower)
            spreading = east + west + upper + lower - 4.0 * q
            target[at(target_field, e), :] = masked(e, q - advect_coef * advected + diffuse_coef * spreading)
        state = buf
        tracer_source, source_field = target, target_field
    return [(buf, 0), (buf, 1), (buf, 2), (tracer_source, source_field)]


def pairs_of(size):
    return [(a, b) for a in range(size) for b in range(a + 1, size)]


def pair_index(pairing_ref):
    size = pairing_ref.shape[0]
    me = lax.axis_index("mem")
    partner = pairing_ref[me]
    low, high = jnp.minimum(me, partner), jnp.maximum(me, partner)
    return low * (2 * size - low - 1) // 2 + high - low - 1


def steps_kernel(size, local_rows, sub, as_rows, *refs):
    extent = local_rows + 2 * HALO
    if as_rows:
        state_ref, factor_ref, out_ref, factor_out, buf, spare = refs
        factor_out[...] = factor_ref[...]
    else:
        state_ref, pairing_ref, out_ref, index_ref, buf, spare = refs
        index_ref[0, 0] = pair_index(pairing_ref)
    lat = lax.axis_index("lat")
    fields = run_steps(state_ref, buf, spare, local_rows, sub, lat * local_rows, local_rows * size)
    for field, (ref, place) in enumerate(fields):
        if not as_rows:
            for tile in range(local_rows * sub // 8):
                column = (field * local_rows * sub // 8 + tile) * TILE
                out_ref[:, column : column + TILE] = ref[pl.ds((place * extent + HALO) * sub + tile * 8, 8), :]
            continue
        for row in range(0, local_rows, 8):
            for t in range(sub):
                first = (place * extent + HALO + row) * sub + t
                out_ref[field, row : row + 8, t * TILE : (t + 1) * TILE] = ref[pl.ds(first, 8, stride=sub), :]


def halo_copies(buf, local_rows, sub, lat, size, send_sem, recv_sem):
    extent = local_rows + 2 * HALO
    mem = lax.axis_index("mem")
    copies = []
    for side, peer in ((0, lat - 1), (1, lat + 1)):
        group = []
        for field in range(FIELDS):
            reach = REACH[field]
            source = HALO if side == 0 else HALO + local_rows - reach
            target = HALO + local_rows if side == 0 else HALO - reach
            group.append(
                pltpu.make_async_remote_copy(
                    src_ref=buf.at[pl.ds((field * extent + source) * sub, reach * sub), :],
                    dst_ref=buf.at[pl.ds((field * extent + target) * sub, reach * sub), :],
                    send_sem=send_sem.at[side, field],
                    recv_sem=recv_sem.at[side, field],
                    device_id=(mem, peer),
                    device_id_type=MESH,
                )
            )
        copies.append(group)
    return copies


def clear_outside(buf, local_rows, sub, lat, size):
    extent = local_rows + 2 * HALO
    zeros = jnp.zeros((HALO * sub, TILE), jnp.float32)

    @pl.when(lat == 0)
    def _():
        for field in range(FIELDS):
            buf[pl.ds(field * extent * sub, HALO * sub), :] = zeros

    @pl.when(lat == size - 1)
    def _():
        for field in range(FIELDS):
            buf[pl.ds((field * extent + HALO + local_rows) * sub, HALO * sub), :] = zeros


def start_halo(copies, lat, size):
    for side, has in ((0, lat > 0), (1, lat < size - 1)):

        @pl.when(has)
        def _(side=side):
            for copy in copies[side]:
                copy.start()


def finish_halo(copies, lat, size):
    for side, has in ((0, lat > 0), (1, lat < size - 1)):

        @pl.when(has)
        def _(side=side):
            for copy in copies[side]:
                copy.wait_send()
            for copy in copies[1 - side]:
                copy.wait_recv()


def planes_from_rows(source, buf, local_rows, sub, fields=range(FIELDS)):
    extent = local_rows + 2 * HALO
    for field in fields:
        for row in range(0, local_rows, 8):
            for t in range(sub):
                first = (field * extent + HALO + row) * sub + t
                buf[pl.ds(first, 8, stride=sub), :] = source[field, row : row + 8, t * TILE : (t + 1) * TILE]


def first_kernel(size, local_rows, sub, x_ref, lab_ref, buf, edge_ref, rows, load_sem, send_sem, recv_sem, lab_send, lab_recv):
    lat = lax.axis_index("lat")
    mem = lax.axis_index("mem")
    barrier = pltpu.get_barrier_semaphore()
    for peer, has in ((lat - 1, lat > 0), (lat + 1, lat < size - 1)):

        @pl.when(has)
        def _(peer=peer):
            pl.semaphore_signal(barrier, inc=1, device_id=(mem, peer), device_id_type=MESH)

    loads = [pltpu.make_async_copy(x_ref.at[f], rows.at[f], load_sem.at[f]) for f in range(FIELDS)]
    for load in loads:
        load.start()
    clear_outside(buf, local_rows, sub, lat, size)
    none = jnp.full((sub, TILE), -1.0, jnp.float32)

    @pl.when(lat == 0)
    def _():
        edge_ref[0] = none

    @pl.when(lat == size - 1)
    def _():
        edge_ref[1] = none

    inner = (lat > 0) & (lat < size - 1)

    @pl.when(inner)
    def _():
        pl.semaphore_wait(barrier, 2)

    @pl.when(jnp.logical_not(inner))
    def _():
        pl.semaphore_wait(barrier, 1)

    copies = halo_copies(buf, local_rows, sub, lat, size, send_sem, recv_sem)
    for side, peer in ((0, lat - 1), (1, lat + 1)):
        row = 0 if side == 0 else local_rows - 1
        copies[side].append(
            pltpu.make_async_remote_copy(
                src_ref=lab_ref.at[row],
                dst_ref=edge_ref.at[1 - side],
                send_sem=lab_send.at[side],
                recv_sem=lab_recv.at[side],
                device_id=(mem, peer),
                device_id_type=MESH,
            )
        )
    for field in range(FIELDS + 1):
        if field < FIELDS:
            loads[field].wait()
            planes_from_rows(rows, buf, local_rows, sub, (field,))
        start_halo([side[field : field + 1] for side in copies], lat, size)
    finish_halo(copies, lat, size)


def second_kernel(
    size, local_rows, sub, first_ref, partner_ref, analysis_ref, lab_ref, edge_ref, buf, factor_ref,
    spread, sums, send_sem, recv_sem, sum_send, sum_recv,
):
    lat = lax.axis_index("lat")
    mem = lax.axis_index("mem")
    extent = local_rows + 2 * HALO
    barrier = pltpu.get_barrier_semaphore()
    for hop in range(1, size):
        pl.semaphore_signal(barrier, inc=1, device_id=(mem, lax.rem(lat + hop, size)), device_id_type=MESH)

    def fold(plane):
        total = plane[0:8]
        for i in range(8, sub, 8):
            total = total + plane[i : i + 8]
        return total

    energies = [jnp.zeros((8, TILE), jnp.float32) for _ in range(REGIONS)]
    counts = [jnp.zeros((8, TILE), jnp.float32) for _ in range(REGIONS)]

    def accumulate(row, carry):
        energies, counts = carry
        total = jnp.zeros((sub, TILE), jnp.float32)
        for field in range(FIELDS):
            parts = []
            for i in range(sub // 8):
                column = ((field * local_rows + row) * (sub // 8) + i) * TILE
                place = pl.ds(pl.multiple_of(column, TILE), TILE)
                parts.append(first_ref[:, place] - partner_ref[:, place])
            half = 0.5 * jnp.concatenate(parts, axis=0)
            spread[field, row] = half
            total = total + half * half
        quarter = 0.125 * total
        here = lab_ref[row]
        before = jnp.where(row == 0, edge_ref[0], lab_ref[jnp.maximum(row - 1, 0)])
        after = jnp.where(row == local_rows - 1, edge_ref[1], lab_ref[jnp.minimum(row + 1, local_rows - 1)])
        new_energies, new_counts = [], []
        for k in range(REGIONS):
            kept = jnp.where(here == k, 1.0, 0.0)
            weight = 2.0 * kept + jnp.where(before == k, 1.0, 0.0) + jnp.where(after == k, 1.0, 0.0)
            new_energies.append(energies[k] + fold(quarter * weight))
            new_counts.append(counts[k] + fold(kept))
        return new_energies, new_counts

    energies, counts = lax.fori_loop(0, local_rows, accumulate, (energies, counts))
    for k in range(REGIONS):
        sums[0, k : k + 1, :] = jnp.sum(energies[k], axis=0, keepdims=True)
        sums[0, REGIONS + k : REGIONS + k + 1, :] = jnp.sum(counts[k], axis=0, keepdims=True)

    pl.semaphore_wait(barrier, size - 1)
    sends = []
    for hop in range(1, size):
        sends.append(
            pltpu.make_async_remote_copy(
                src_ref=sums.at[0],
                dst_ref=sums.at[hop],
                send_sem=sum_send.at[hop],
                recv_sem=sum_recv.at[hop],
                device_id=(mem, lax.rem(lat + hop, size)),
                device_id_type=MESH,
            )
        )
    for copy in sends:
        copy.start()
    clear_outside(buf, local_rows, sub, lat, size)
    planes_from_rows(analysis_ref, buf, local_rows, sub)
    for copy in sends:
        copy.wait()
    total = sums[0]
    for hop in range(1, size):
        total = total + sums[hop]
    total = jnp.sum(total, axis=1, keepdims=True)
    factor = target_size / jnp.sqrt(total[:REGIONS] / total[REGIONS:] + small_eps)
    wide = jnp.broadcast_to(factor, (REGIONS, TILE))
    diagonal = lax.broadcasted_iota(jnp.int32, (REGIONS, TILE), 0) == lax.broadcasted_iota(
        jnp.int32, (REGIONS, TILE), 1
    )
    factor_ref[...] = jnp.sum(jnp.where(diagonal, wide, 0.0), axis=0, keepdims=True)[:, :REGIONS]
    lanes = [jnp.broadcast_to(wide[k : k + 1], (sub, TILE)) for k in range(REGIONS)]

    def middle(row, carry):
        here = lab_ref[row]
        scale = lanes[0]
        for k in range(1, REGIONS):
            scale = jnp.where(here == k, lanes[k], scale)
        for field in range(FIELDS):
            place = pl.ds(pl.multiple_of((field * extent + HALO + row) * sub, sub), sub)
            buf[place, :] = buf[place, :] + scale * spread[field, row]
        return carry

    lax.fori_loop(0, local_rows, middle, 0)
    copies = halo_copies(buf, local_rows, sub, lat, size, send_sem, recv_sem)
    start_halo(copies, lat, size)
    finish_halo(copies, lat, size)


def partner_fields(fields, pairing, index):
    pairs = pairs_of(lax.axis_size("mem"))
    if len(pairs) > MAX_BRANCHES:
        piece = lax.all_gather(fields, "mem", axis=0)
        return lax.dynamic_index_in_dim(piece, pairing[lax.axis_index("mem")], 0, keepdims=False)
    branches = [
        functools.partial(lax.ppermute, axis_name="mem", perm=[(a, b), (b, a)]) for a, b in pairs
    ]
    return lax.switch(index, branches, fields)


def local(replica_variables, analysis, labels, pairing):
    size = lax.axis_size("lat")
    fields, local_rows, width = analysis.shape
    sub = width // TILE
    extent = local_rows + 2 * HALO
    wide = jax.ShapeDtypeStruct((8, fields * local_rows * width // 8), jnp.float32)
    extended = jax.ShapeDtypeStruct((fields * extent * sub, TILE), jnp.float32)
    edges = jax.ShapeDtypeStruct((2, sub, TILE), jnp.float32)
    factors = jax.ShapeDtypeStruct((1, REGIONS), jnp.float32)
    label_planes = jnp.broadcast_to(labels.astype(jnp.float32)[..., None], (local_rows, sub, TILE))
    whole = pl.BlockSpec(memory_space=pltpu.VMEM)
    buffers = [
        pltpu.VMEM((fields * extent * sub, TILE), jnp.float32),
        pltpu.VMEM((extent * sub, TILE), jnp.float32),
    ]
    halo_sems = [pltpu.SemaphoreType.DMA((2, fields)), pltpu.SemaphoreType.DMA((2, fields))]
    state, edge = pl.pallas_call(
        functools.partial(first_kernel, size, local_rows, sub),
        out_shape=(extended, edges),
        in_specs=[pl.BlockSpec(memory_space=pltpu.HBM), whole],
        out_specs=(whole, whole),
        scratch_shapes=[pltpu.VMEM(analysis.shape, jnp.float32), pltpu.SemaphoreType.DMA((fields,))]
        + halo_sems
        + [pltpu.SemaphoreType.DMA((2,)), pltpu.SemaphoreType.DMA((2,))],
        compiler_params=pltpu.CompilerParams(collective_id=0, has_side_effects=True, vmem_limit_bytes=VMEM_LIMIT),
    )(replica_variables[0], label_planes)
    smem = pl.BlockSpec(memory_space=pltpu.SMEM)
    first, index = pl.pallas_call(
        functools.partial(steps_kernel, size, local_rows, sub, False),
        out_shape=(wide, jax.ShapeDtypeStruct((1, 1), jnp.int32)),
        in_specs=[whole, smem],
        out_specs=(whole, smem),
        scratch_shapes=buffers,
        compiler_params=pltpu.CompilerParams(vmem_limit_bytes=VMEM_LIMIT),
    )(state, pairing)
    partner = partner_fields(first, pairing, index[0, 0])
    state, factor = pl.pallas_call(
        functools.partial(second_kernel, size, local_rows, sub),
        out_shape=(extended, factors),
        in_specs=[whole] * 5,
        out_specs=(whole, whole),
        scratch_shapes=[
            pltpu.VMEM((fields, local_rows, sub, TILE), jnp.float32),
            pltpu.VMEM((size, 2 * REGIONS, TILE), jnp.float32),
        ]
        + halo_sems
        + [pltpu.SemaphoreType.DMA((size,)), pltpu.SemaphoreType.DMA((size,))],
        compiler_params=pltpu.CompilerParams(collective_id=1, has_side_effects=True, vmem_limit_bytes=VMEM_LIMIT),
    )(first, partner, analysis, label_planes, edge)
    closing, factor = pl.pallas_call(
        functools.partial(steps_kernel, size, local_rows, sub, True),
        out_shape=(jax.ShapeDtypeStruct(analysis.shape, jnp.float32), factors),
        in_specs=[whole] * 2,
        out_specs=(whole, whole),
        scratch_shapes=buffers,
        compiler_params=pltpu.CompilerParams(vmem_limit_bytes=VMEM_LIMIT),
    )(state, factor)
    return (closing[None], factor)


CLASS_ID = 2
ORDER = (2, 1, 0, 3)
COLUMNS = 2
CHUNKS = 2
PAIR_VMEM = 24 * 2**20


def matchings(items):
    if not items:
        return [()]
    head, found = items[0], []
    for i in range(1, len(items)):
        for rest in matchings(items[1:i] + items[i + 1 :]):
            found.append(((head, items[i]),) + rest)
    return found


def level_edges(matching):
    return tuple(sorted(tuple(sorted((a // COLUMNS, b // COLUMNS))) for a, b in matching))


def level_patterns(size):
    return sorted({level_edges(m) for m in matchings(tuple(range(size)))})


def slot_tables(edges, levels):
    peer = [[z, z] for z in range(levels)]
    slot = [[0, 1] for _ in range(levels)]
    moves = [0] * levels
    used = [0] * levels
    for a, b in edges:
        if a == b:
            continue
        i, j = used[a], used[b]
        used[a] += 1
        used[b] += 1
        peer[a][i], slot[a][i] = b, j
        peer[b][j], slot[b][j] = a, i
        moves[a] = moves[b] = 1
    return peer, slot, moves


def pattern_index(patterns, pairing_ref):
    members = pairing_ref.shape[0]
    levels = members // COLUMNS
    level = [lax.div(pairing_ref[m], COLUMNS) for m in range(members)]
    count = {}
    for a in range(levels):
        for b in range(a + 1, levels):
            count[a, b] = sum(jnp.where(level[a * COLUMNS + i] == b, 1, 0) for i in range(COLUMNS))
    index = jnp.int32(0)
    for k, edges in enumerate(patterns):
        good = None
        for pair, n in count.items():
            same = n == sum(e == pair for e in edges)
            good = same if good is None else good & same
        index = jnp.where(good, k, index)
    return index


def lookup(index, table):
    value = jnp.int32(table[0])
    for k, entry in enumerate(table):
        if k and entry != table[0]:
            value = jnp.where(index == k, entry, value)
    return value


class Flow:
    def __init__(self, local_rows, sub, start, rows_all):
        self.local_rows, self.sub, self.start, self.rows_all = local_rows, sub, start, rows_all
        self.extent = local_rows + 2 * HALO

    def at(self, field, e):
        return pl.ds((field * self.extent + e) * self.sub, self.sub)

    def owns(self, e):
        return HALO <= e < HALO + self.local_rows

    def masked(self, e, values):
        if self.owns(e):
            return values
        row = self.start + (e - HALO)
        return jnp.where((row >= 0) & (row < self.rows_all), 1.0, 0.0).astype(jnp.float32) * values

    def height(self, source, e):
        divergence = diff_lon(source[self.at(1, e), :]) + source[self.at(2, e + 1), :] - source[self.at(2, e - 1), :]
        return self.masked(e, source[self.at(0, e), :] - depth_coef * divergence)

    def wind(self, source, heights, e):
        row = (self.start + (e - HALO)).astype(jnp.float32)
        f = coriolis_coef * (2.0 * (row + 0.5) / self.rows_all - 1.0)
        v = source[self.at(2, e), :]
        u1 = source[self.at(1, e), :] + f * v - grav_coef * diff_lon(heights[self.at(0, e), :])
        slope = heights[self.at(0, e + 1), :] - heights[self.at(0, e - 1), :]
        return u1, self.masked(e, v - f * u1 - grav_coef * slope)

    def tracer(self, source, place, u1, v1, e):
        q = source[self.at(place, e), :]
        upper, lower = source[self.at(place, e + 1), :], source[self.at(place, e - 1), :]
        east, west = shift_lon(q)
        advected = u1 * (east - west) + v1 * (upper - lower)
        spreading = east + west + upper + lower - 4.0 * q
        return self.masked(e, q - advect_coef * advected + diffuse_coef * spreading)


def flow_steps(flow, state, buf, spare, keep, flow_halo, tracer_halo, flow_done):
    low, high = HALO, HALO + flow.local_rows
    source, place, tracer_source = state, 3, state
    for step in range(STEPS):
        margin = 2 * (STEPS - 1 - step)
        narrow = STEPS - 1 - step
        last = step == STEPS - 1
        target, spot = (spare, 0) if step % 2 == 0 else (buf, 3)

        def heights(rows, source=source, last=last):
            for e in rows:
                value = flow.height(source, e)
                buf[flow.at(0, e), :] = value
                if last and keep is not None and flow.owns(e):
                    keep(0, e, value)

        def winds(rows, source=source, last=last):
            for e in rows:
                u1, v1 = flow.wind(source, buf, e)
                buf[flow.at(1, e), :] = u1
                buf[flow.at(2, e), :] = v1
                if last and keep is not None:
                    keep(1, e, u1)
                    keep(2, e, v1)

        def tracers(rows, last=last, tracer_source=tracer_source, place=place, target=target, spot=spot):
            for e in rows:
                value = flow.tracer(tracer_source, place, buf[flow.at(1, e), :], buf[flow.at(2, e), :], e)
                if last and keep is not None:
                    keep(3, e, value)
                else:
                    target[flow.at(spot, e), :] = value

        def run(piece, lower, upper, inner):
            if inner is None:
                piece(range(lower, upper))
            else:
                piece(range(lower, inner[0]))
                piece(range(inner[1], upper))

        early = step == 0 and flow_halo is not None
        inner = [None] * 3
        if early:
            inner = [(low + 1, high - 1), (low + 2, high - 2), (low + 2, high - 2)]
            for piece, rows in zip((heights, winds, tracers), inner):
                piece(range(*rows))
            flow_halo()
        run(heights, low - margin - 1, high + margin + 1, inner[0])
        run(winds, low - margin, high + margin, inner[1])
        if early:
            tracer_halo()
        if last and flow_done is not None:
            flow_done()
        run(tracers, low - narrow, high + narrow, inner[2])
        source, tracer_source, place = buf, target, spot
    return tracer_source, place


def opening_kernel(
    size, local_rows, sub, patterns, x_ref, pairing_ref, out_ref, index_ref,
    state, buf, spare, rows, load_sem, send_sem, recv_sem,
):
    lat = lax.axis_index("lat")
    mem = lax.axis_index("mem")
    even = lax.rem(lat, 2) == 0
    odd = jnp.logical_not(even)
    barrier = pltpu.get_barrier_semaphore()
    mate = lat + 1 - 2 * lax.rem(lat, 2)
    pl.semaphore_signal(barrier, inc=1, device_id=(mem, mate), device_id_type=MESH)
    loads = [pltpu.make_async_copy(x_ref.at[f], rows.at[f], load_sem.at[f]) for f in range(FIELDS)]
    for f in ORDER:
        loads[f].start()
    index_ref[0, 0] = pattern_index(patterns, pairing_ref)
    extent = local_rows + 2 * HALO
    zeros = jnp.zeros((HALO * sub, TILE), jnp.float32)
    for has, place in ((even, 0), (odd, HALO + local_rows)):

        @pl.when(has)
        def _(place=place):
            for field in range(FIELDS):
                state[pl.ds((field * extent + place) * sub, HALO * sub), :] = zeros

    pl.semaphore_wait(barrier, 1)
    copies = halo_copies(state, local_rows, sub, lat, size, send_sem, recv_sem)
    sides = ((0, odd), (1, even))
    for f in ORDER:
        loads[f].wait()
        planes_from_rows(rows, state, local_rows, sub, (f,))
        for side, has in sides:

            @pl.when(has)
            def _(side=side, f=f):
                copies[side][f].start()

    def received(fields):
        for side, has in sides:

            @pl.when(has)
            def _(side=side):
                for f in fields:
                    copies[1 - side][f].wait_recv()

    def keep(field, e, value):
        out_ref[pl.ds((field * local_rows + e - HALO) * sub, sub), :] = value

    flow = Flow(local_rows, sub, lat * local_rows, local_rows * size)
    flow_steps(flow, state, buf, spare, keep, lambda: received(ORDER[:3]), lambda: received(ORDER[3:]), None)
    for side, has in sides:

        @pl.when(has)
        def _(side=side):
            for copy in copies[side]:
                copy.wait_send()


def plane(sub, index):
    return pl.ds(pl.multiple_of(index * sub, sub), sub)


def fold(block):
    total = block[0:8]
    for i in range(8, block.shape[0], 8):
        total = total + block[i : i + 8]
    return total


def pair_kernel(
    tables, size, local_rows, sub,
    given_ref, x_ref, analysis_ref, lab_ref, pairing_ref,
    state, factor_ref,
    first_ref, raw, lab_near, xv, av, near, send, came, onward, final, spread, labels, weights, energy, tally, sums,
    load_sem, near_send, near_recv, z_send, z_recv, last_send, last_recv,
    raw_send, raw_recv, ana_send, ana_recv, lab_send, lab_recv, halo_send, halo_recv, sum_send, sum_recv,
):
    lat = lax.axis_index("lat")
    mem = lax.axis_index("mem")
    z, y = lax.div(mem, COLUMNS), lax.rem(mem, COLUMNS)
    peer_table, slot_table, moves_table = tables
    levels = len(moves_table)
    half = local_rows // COLUMNS
    deep = half // CHUNKS
    block = deep * sub
    chunks = FIELDS * CHUNKS
    extent = local_rows + 2 * HALO
    other = (z * COLUMNS + 1 - y, lat)
    peers = [lookup(z, [peer_table[k][j] for k in range(levels)]) for j in range(2)]
    slots = [lookup(z, [slot_table[k][j] for k in range(levels)]) for j in range(2)]
    moves = lookup(z, moves_table) == 1

    copy_first = pltpu.make_async_copy(given_ref, first_ref, load_sem.at[0])
    copy_first.start()
    load_x = pltpu.make_async_copy(x_ref, xv, load_sem.at[1])
    load_x.start()
    load = pltpu.make_async_copy(analysis_ref, av, load_sem.at[2])
    load.start()
    even = lax.rem(lat, 2) == 0
    far = ((0, even & (lat > 0)), (1, jnp.logical_not(even) & (lat < size - 1)))
    has_far = far[0][1] | far[1][1]
    early = chunks // 2
    barrier = pltpu.get_barrier_semaphore()
    pl.semaphore_signal(barrier, inc=1, device_id=other, device_id_type=MESH)

    @pl.when(moves)
    def _():
        for j in range(2):
            pl.semaphore_signal(barrier, inc=1, device_id=(peers[j] * COLUMNS + y, lat), device_id_type=MESH)

    for hop in range(1, size):
        pl.semaphore_signal(barrier, inc=1, device_id=(mem, lax.rem(lat + hop, size)), device_id_type=MESH)
    clear_outside(state, local_rows, sub, lat, size)
    clear_outside(spread, local_rows, sub, lat, size)
    none = jnp.full((HALO * sub, TILE), -1.0, jnp.float32)

    @pl.when(lat == 0)
    def _():
        labels[pl.ds(0, HALO * sub), :] = none

    @pl.when(lat == size - 1)
    def _():
        labels[pl.ds((HALO + local_rows) * sub, HALO * sub), :] = none

    @pl.when(moves)
    def _():
        pl.semaphore_wait(barrier, size + 2)

    @pl.when(jnp.logical_not(moves))
    def _():
        pl.semaphore_wait(barrier, size)

    def row_of(part, column):
        place = jnp.where(even, CHUNKS - 1 - part, part)
        return (place * COLUMNS + column) * deep

    def rows_of(c, column):
        part, field = lax.div(c, FIELDS), lax.rem(c, FIELDS)
        return pl.ds(pl.multiple_of((field * local_rows + row_of(part, column)) * sub, sub), block)

    def near_copy(c):
        return pltpu.make_async_remote_copy(
            src_ref=first_ref.at[rows_of(c, 1 - y), :],
            dst_ref=near.at[c],
            send_sem=near_send.at[c],
            recv_sem=near_recv.at[c],
            device_id=other,
            device_id_type=MESH,
        )

    def cross_copy(c, j, slot):
        return pltpu.make_async_remote_copy(
            src_ref=send.at[j, c],
            dst_ref=came.at[slot, c],
            send_sem=z_send.at[j, c],
            recv_sem=z_recv.at[slot, c],
            device_id=(peers[j] * COLUMNS + y, lat),
            device_id_type=MESH,
        )

    def last_copy(c):
        return pltpu.make_async_remote_copy(
            src_ref=onward.at[c],
            dst_ref=final.at[c],
            send_sem=last_send.at[c],
            recv_sem=last_recv.at[c],
            device_id=other,
            device_id_type=MESH,
        )

    def halo_copy(field, reach, side, peer):
        source = HALO if side == 0 else HALO + local_rows - reach
        target = HALO + local_rows if side == 0 else HALO - reach
        return pltpu.make_async_remote_copy(
            src_ref=spread.at[pl.ds(pl.multiple_of((field * extent + source) * sub, sub), reach * sub), :],
            dst_ref=spread.at[pl.ds(pl.multiple_of((field * extent + target) * sub, sub), reach * sub), :],
            send_sem=halo_send.at[side, field],
            recv_sem=halo_recv.at[side, field],
            device_id=(mem, peer),
            device_id_type=MESH,
        )

    def start_near(c, carry):
        near_copy(c).start()
        return carry

    copy_first.wait()
    lax.fori_loop(0, early, start_near, 0)
    raw_copies = halo_copies(raw, local_rows, sub, lat, size, raw_send, raw_recv)
    load_x.wait()

    @pl.when(has_far)
    def _():
        def put(index, carry):
            field, tile = lax.div(index, sub), lax.rem(index, sub)
            for row in range(0, local_rows, 8):
                raw[pl.ds((field * extent + HALO + row) * sub + tile, 8, stride=sub), :] = xv[
                    field, row : row + 8, pl.ds(pl.multiple_of(tile * TILE, TILE), TILE)
                ]
            return carry

        lax.fori_loop(0, FIELDS * sub, put, 0, unroll=4)

    for side, has in far:

        @pl.when(has)
        def _(side=side):
            for f in ORDER:
                raw_copies[side][f].start()

    pick = [pairing_ref[z * COLUMNS + i] for i in range(COLUMNS)]
    pick_level = [lax.div(p, COLUMNS) for p in pick]
    first_slot_item = jnp.where(pick_level[0] == peers[0], 0, 1)
    here_level = jnp.where(y == 0, pick_level[0], pick_level[1])
    here_column = lax.rem(jnp.where(y == 0, pick[0], pick[1]), COLUMNS)
    keep_slot = jnp.where(peers[0] == peers[1], here_column, jnp.where(here_level == peers[0], 0, 1))
    own_first = jnp.full((sub, TILE), first_slot_item, jnp.int32) == y
    keep_first = jnp.full((sub, TILE), keep_slot, jnp.int32) == 0
    diagonal = lax.broadcasted_iota(jnp.int32, (sub, sub), 0) == lax.broadcasted_iota(jnp.int32, (sub, sub), 1)

    lab_copies = [
        [
            pltpu.make_async_remote_copy(
                src_ref=lab_ref,
                dst_ref=lab_near.at[1 - side],
                send_sem=lab_send.at[side],
                recv_sem=lab_recv.at[side],
                device_id=(mem, peer),
                device_id_type=MESH,
            )
        ]
        for side, peer in ((0, lat - 1), (1, lat + 1))
    ]
    start_halo(lab_copies, lat, size)

    def label_rows(source, first, lower, count):
        def label_row(i, carry):
            line = jnp.broadcast_to(source[pl.ds(first + i, 1), :].astype(jnp.float32), (sub, sub))
            column = jnp.sum(jnp.where(diagonal, line, 0.0), axis=1, keepdims=True)
            labels[plane(sub, lower + i), :] = jnp.broadcast_to(column, (sub, TILE))
            return carry

        lax.fori_loop(0, count, label_row, 0, unroll=2)

    label_rows(lab_ref, 0, HALO, local_rows)
    finish_halo(lab_copies, lat, size)

    @pl.when(lat > 0)
    def _():
        label_rows(lab_near.at[0], local_rows - HALO, 0, HALO)

    @pl.when(lat < size - 1)
    def _():
        label_rows(lab_near.at[1], 0, HALO + local_rows, HALO)

    def weigh(row, counts):
        here = labels[plane(sub, HALO + row), :]
        before = labels[plane(sub, HALO + row - 1), :]
        after = labels[plane(sub, HALO + row + 1), :]
        new = []
        for k in range(REGIONS):
            kept = jnp.where(here == k, 1.0, 0.0)
            around = jnp.where(before == k, 0.125, 0.0) + jnp.where(after == k, 0.125, 0.0)
            weights[k, plane(sub, row), :] = 0.25 * kept + around
            new.append(counts[k] + fold(kept))
        return new

    counts = lax.fori_loop(0, local_rows, weigh, [jnp.zeros((8, TILE), jnp.float32) for _ in range(REGIONS)])
    for k in range(REGIONS):
        tally[pl.ds(k * 8, 8), :] = counts[k]
    energy[...] = jnp.zeros_like(energy)

    load.wait()
    tiles = FIELDS * sub // chunks

    def lay_out(c):
        for i in range(tiles):
            index = c * tiles + i
            field, tile = lax.div(index, sub), lax.rem(index, sub)
            for row in range(0, local_rows, 8):
                state[pl.ds((field * extent + HALO + row) * sub + tile, 8, stride=sub), :] = av[
                    field, row : row + 8, pl.ds(pl.multiple_of(tile * TILE, TILE), TILE)
                ]

    ana_copies = halo_copies(state, local_rows, sub, lat, size, ana_send, ana_recv)

    def cross(c, carry):
        near_copy(c).wait_recv()

        @pl.when(moves)
        def _():
            start = rows_of(c, y).start
            for r in range(deep):
                here = pl.ds(r * sub, sub)
                a = first_ref[pl.ds(pl.multiple_of(start + r * sub, sub), sub), :]
                b = near[c, here, :]
                send[0, c, here, :] = jnp.where(own_first, a, b)
                send[1, c, here, :] = jnp.where(own_first, b, a)
            for j in range(2):
                cross_copy(c, j, slots[j]).start()

        lay_out(c)

        @pl.when(c == chunks - 1)
        def _():
            start_halo(ana_copies, lat, size)

        return carry

    def late_rows():
        base = jnp.where(even, HALO, local_rows)

        def at(field, e):
            return plane(sub, field * extent + e)

        def two(piece, first, count):
            def both(i, carry):
                for k in range(2):
                    piece(first + 2 * i + k)
                return carry

            lax.fori_loop(0, lax.div(count, 2), both, 0)

        def step_rows(step, carry):
            margin = 2 * (STEPS - 1 - step)
            narrow = STEPS - 1 - step
            place = FIELDS - 1 + lax.rem(step, 2)
            spot = FIELDS - lax.rem(step, 2)

            def height(e):
                divergence = diff_lon(raw[at(1, e), :]) + raw[at(2, e + 1), :] - raw[at(2, e - 1), :]
                raw[at(0, e), :] = raw[at(0, e), :] - depth_coef * divergence

            def wind(e):
                row = (lat * local_rows + e - HALO).astype(jnp.float32)
                f = coriolis_coef * (2.0 * (row + 0.5) / (local_rows * size) - 1.0)
                v = raw[at(2, e), :]
                u1 = raw[at(1, e), :] + f * v - grav_coef * diff_lon(raw[at(0, e), :])
                slope = raw[at(0, e + 1), :] - raw[at(0, e - 1), :]
                raw[at(1, e), :] = u1
                raw[at(2, e), :] = v - f * u1 - grav_coef * slope

            def tracer(e):
                q = raw[at(place, e), :]
                upper, lower = raw[at(place, e + 1), :], raw[at(place, e - 1), :]
                east, west = shift_lon(q)
                advected = raw[at(1, e), :] * (east - west) + raw[at(2, e), :] * (upper - lower)
                spreading = east + west + upper + lower - 4.0 * q
                raw[at(spot, e), :] = q - advect_coef * advected + diffuse_coef * spreading

            two(height, base - margin - 1, HALO + 2 * margin + 2)
            two(wind, base - margin, HALO + 2 * margin)
            two(tracer, base - narrow, HALO + 2 * narrow)
            return carry

        lax.fori_loop(0, STEPS, step_rows, 0)
        for field, spot in enumerate((0, 1, 2, FIELDS - (STEPS - 1) % 2)):
            first_ref[pl.ds(pl.multiple_of((field * local_rows + base - HALO) * sub, sub), HALO * sub), :] = raw[
                pl.ds(pl.multiple_of((spot * extent + base) * sub, sub), HALO * sub), :
            ]

    lax.fori_loop(0, early, cross, 0)
    for side, has in far:

        @pl.when(has)
        def _(side=side):
            for copy in raw_copies[side]:
                copy.wait_send()
            for copy in raw_copies[1 - side]:
                copy.wait_recv()

    @pl.when(has_far)
    def _():
        late_rows()

    lax.fori_loop(early, chunks, start_near, 0)

    def pass_on(c):
        @pl.when(moves)
        def _():
            for j in range(2):
                cross_copy(c, j, j).wait_recv()
            for r in range(deep):
                here = pl.ds(r * sub, sub)
                a = came[0, c, here, :]
                b = came[1, c, here, :]
                onward[c, here, :] = jnp.where(keep_first, b, a)
                near[c, here, :] = jnp.where(keep_first, a, b)

        @pl.when(jnp.logical_not(moves))
        def _():
            onward[c] = first_ref[rows_of(c, y), :]

        last_copy(c).start()

    def absorb(field, first_row, theirs):
        totals = [energy[pl.ds(k * 8, 8), :] for k in range(REGIONS)]
        for r in range(deep):
            row = first_row + r
            value = 0.5 * (first_ref[plane(sub, field * local_rows + row), :] - theirs[r * sub : (r + 1) * sub, :])
            spread[plane(sub, field * extent + HALO + row), :] = value
            square = value * value
            for k in range(REGIONS):
                totals[k] = totals[k] + fold(square * weights[k, plane(sub, row), :])
        for k in range(REGIONS):
            energy[pl.ds(k * 8, 8), :] = totals[k]

    def arrive(field, part):
        c = part * FIELDS + field
        last_copy(c).wait_recv()
        absorb(field, row_of(part, 1 - y), final.at[c])

    sides = ((0, lat - 1, lat > 0), (1, lat + 1, lat < size - 1))

    def send_halo(field, reach):
        for side, peer, has in sides:

            @pl.when(has)
            def _(side=side, peer=peer):
                halo_copy(field, reach, side, peer).start()

    def take(c, carry):
        part, field = lax.div(c, FIELDS), lax.rem(c, FIELDS)
        arrive(field, part)

        @pl.when((part == CHUNKS - 1) & (field < FIELDS - 1))
        def _():
            send_halo(field, HALO)

        return carry

    caught_up = early + 1

    def stage(c, carry):
        @pl.when(c < chunks)
        def _():
            pass_on(c)

        @pl.when(c < early)
        def _():
            cross(c + early, 0)

        @pl.when(c < chunks)
        def _():
            absorb(lax.rem(c, FIELDS), row_of(lax.div(c, FIELDS), y), near.at[c])

        done = jnp.where(c > caught_up, c - 1, 0)
        lax.fori_loop(done, jnp.where(c >= caught_up, c, 0), take, 0)
        return carry

    lax.fori_loop(0, chunks + 1, stage, 0)
    for k in range(REGIONS):
        for i, table in enumerate((energy, tally)):
            sums[0, i * REGIONS + k : i * REGIONS + k + 1, :] = jnp.sum(
                table[pl.ds(k * 8, 8), :], axis=0, keepdims=True
            )
    shares = [
        pltpu.make_async_remote_copy(
            src_ref=sums.at[0],
            dst_ref=sums.at[hop],
            send_sem=sum_send.at[hop],
            recv_sem=sum_recv.at[hop],
            device_id=(mem, lax.rem(lat + hop, size)),
            device_id_type=MESH,
        )
        for hop in range(1, size)
    ]
    for copy in shares:
        copy.start()
    send_halo(FIELDS - 1, REACH[FIELDS - 1])
    finish_halo(ana_copies, lat, size)

    def finish(c, carry):
        near_copy(c).wait_send()
        last_copy(c).wait_send()

        @pl.when(moves)
        def _():
            for j in range(2):
                cross_copy(c, j, j).wait_send()

        return carry

    lax.fori_loop(0, chunks, finish, 0)
    for copy in shares:
        copy.wait()
    total = sums[0]
    for hop in range(1, size):
        total = total + sums[hop]
    total = jnp.sum(total, axis=1, keepdims=True)
    factor = target_size / jnp.sqrt(total[:REGIONS] / total[REGIONS:] + small_eps)
    wide = jnp.broadcast_to(factor, (REGIONS, TILE))
    corner = lax.broadcasted_iota(jnp.int32, (REGIONS, TILE), 0) == lax.broadcasted_iota(
        jnp.int32, (REGIONS, TILE), 1
    )
    factor_ref[...] = jnp.sum(jnp.where(corner, wide, 0.0), axis=0, keepdims=True)[:, :REGIONS]
    lanes = [jnp.broadcast_to(wide[k : k + 1], (sub, TILE)) for k in range(REGIONS)]

    def middle(e, carry):
        here = labels[plane(sub, e), :]
        scale = lanes[0]
        for k in range(1, REGIONS):
            scale = jnp.where(here == k, lanes[k], scale)
        for field in range(FIELDS):
            place = plane(sub, field * extent + e)
            state[place, :] = state[place, :] + scale * spread[place, :]
        return carry

    lax.fori_loop(HALO, HALO + local_rows, middle, 0, unroll=2)
    for field in range(FIELDS):
        reach = REACH[field] if field == FIELDS - 1 else HALO
        for side, peer, has in sides:

            @pl.when(has)
            def _(field=field, reach=reach, side=side, peer=peer):
                halo_copy(field, reach, side, peer).wait_send()
                halo_copy(field, reach, 1 - side, peer).wait_recv()

    lax.fori_loop(0, HALO, middle, 0, unroll=2)
    lax.fori_loop(HALO + local_rows, extent, middle, 0, unroll=2)


def pair_call(tables, index, size, fields, local_rows, width):
    sub = width // TILE
    half = local_rows // COLUMNS
    chunks = fields * CHUNKS
    block = half // CHUNKS * sub
    extent = local_rows + 2 * HALO
    f32 = jnp.float32
    vmem = lambda *shape: pltpu.VMEM(shape, f32)
    pair = lambda *shape: [pltpu.SemaphoreType.DMA(shape)] * 2
    whole = pl.BlockSpec(memory_space=pltpu.VMEM)
    hbm = pl.BlockSpec(memory_space=pltpu.HBM)
    return pl.pallas_call(
        functools.partial(pair_kernel, tables, size, local_rows, sub),
        out_shape=(
            jax.ShapeDtypeStruct((fields * extent * sub, TILE), f32),
            jax.ShapeDtypeStruct((1, REGIONS), f32),
        ),
        in_specs=[whole, hbm, hbm, whole, pl.BlockSpec(memory_space=pltpu.SMEM)],
        out_specs=(whole, whole),
        scratch_shapes=[
            vmem(fields * local_rows * sub, TILE),
            vmem((fields + 1) * extent * sub, TILE),
            pltpu.VMEM((2, local_rows, sub), jnp.int32),
            vmem(fields, local_rows, width),
            vmem(fields, local_rows, width),
            vmem(chunks, block, TILE),
            vmem(2, chunks, block, TILE),
            vmem(2, chunks, block, TILE),
            vmem(chunks, block, TILE),
            vmem(chunks, block, TILE),
            vmem(fields * extent * sub, TILE),
            vmem(extent * sub, TILE),
            vmem(REGIONS, local_rows * sub, TILE),
            vmem(REGIONS * 8, TILE),
            vmem(REGIONS * 8, TILE),
            vmem(size, 2 * REGIONS, TILE),
            pltpu.SemaphoreType.DMA((3,)),
        ]
        + pair(chunks)
        + pair(2, chunks)
        + pair(chunks)
        + pair(2, fields)
        + pair(2, fields)
        + pair(2)
        + pair(2, fields)
        + pair(size),
        compiler_params=pltpu.CompilerParams(
            collective_id=CLASS_ID + index, has_side_effects=True, vmem_limit_bytes=PAIR_VMEM
        ),
    )


def cycle(replica_variables, analysis, labels, pairing):
    size = lax.axis_size("lat")
    members = lax.axis_size("mem")
    fields, local_rows, width = analysis.shape
    sub = width // TILE
    extent = local_rows + 2 * HALO
    inner = jax.ShapeDtypeStruct((fields * local_rows * sub, TILE), jnp.float32)
    factors = jax.ShapeDtypeStruct((1, REGIONS), jnp.float32)
    patterns = level_patterns(members)
    whole = pl.BlockSpec(memory_space=pltpu.VMEM)
    smem = pl.BlockSpec(memory_space=pltpu.SMEM)
    halo_sems = [pltpu.SemaphoreType.DMA((2, fields)), pltpu.SemaphoreType.DMA((2, fields))]
    buffers = [
        pltpu.VMEM((fields * extent * sub, TILE), jnp.float32),
        pltpu.VMEM((extent * sub, TILE), jnp.float32),
    ]
    x = pltpu.with_memory_space_constraint(replica_variables[0], pltpu.HBM)
    first, index = pl.pallas_call(
        functools.partial(opening_kernel, size, local_rows, sub, patterns),
        out_shape=(inner, jax.ShapeDtypeStruct((1, 1), jnp.int32)),
        in_specs=[pl.BlockSpec(memory_space=pltpu.HBM), smem],
        out_specs=(whole, smem),
        scratch_shapes=[pltpu.VMEM((fields * extent * sub, TILE), jnp.float32)]
        + buffers
        + [pltpu.VMEM(analysis.shape, jnp.float32), pltpu.SemaphoreType.DMA((fields,))]
        + halo_sems,
        compiler_params=pltpu.CompilerParams(collective_id=0, has_side_effects=True, vmem_limit_bytes=PAIR_VMEM),
    )(x, pairing)
    branches = [
        pair_call(slot_tables(edges, members // COLUMNS), k, size, fields, local_rows, width)
        for k, edges in enumerate(patterns)
    ]
    state, factor = lax.switch(
        index[0, 0], branches, first, x, pltpu.with_memory_space_constraint(analysis, pltpu.HBM), labels, pairing
    )
    closing, factor = pl.pallas_call(
        functools.partial(steps_kernel, size, local_rows, sub, True),
        out_shape=(jax.ShapeDtypeStruct(analysis.shape, jnp.float32), factors),
        in_specs=[whole] * 2,
        out_specs=(whole, whole),
        scratch_shapes=buffers,
        compiler_params=pltpu.CompilerParams(vmem_limit_bytes=VMEM_LIMIT),
    )(state, factor)
    return (closing[None], factor)


def either(replica_variables, analysis, labels, pairing):
    members, rows = lax.axis_size("mem"), analysis.shape[1]
    levels = members // COLUMNS
    fits = members % COLUMNS == 0 and 2 <= levels <= MAX_LEVELS
    if fits and rows == 8 * COLUMNS and rows % (FIELDS * CHUNKS) == 0 and lax.axis_size("lat") % 2 == 0:
        return cycle(replica_variables, analysis, labels, pairing)
    return local(replica_variables, analysis, labels, pairing)


def solution(mesh):
    return jax.shard_map(
        either,
        mesh=mesh,
        in_specs=(P("mem", None, "lat", None), P(None, "lat", None), P("lat", None), P()),
        out_specs=(P("mem", None, "lat", None), P("mem", None)),
        check_vma=False,
    )
```
